256 devices in a mesh: shot: 4 (over y_lo, core), dom: 64 (over x, y_hi, z).
Axes of the slice: x: 4, y: 4 (y_hi: 2, y_lo: 2; y = y_hi * 2 + y_lo), z: 8, core: 2. Of those that a mesh axis runs over, the one named last changes fastest.
Arguments:
- wave_before: float32 [4, 1024, 64, 256], P('shot', 'dom'), may hold values from -1.5 to 1.5
- wave_current: float32 [4, 1024, 64, 256], P('shot', 'dom'), may hold values from -1.5 to 1.5
- adjoint_far: float32 [4, 1024, 64, 256], P('shot', 'dom'), may hold values from -1.5 to 1.5
- adjoint_near: float32 [4, 1024, 64, 256], P('shot', 'dom'), may hold values from -1.5 to 1.5
- labels: int32 [1024, 64, 256], P('dom'), may hold values from 0 to 7
- table: float32 [8], replicated, may hold values from 0.03 to 0.12
- source_index: int32 [4, 3], P('shot'), may hold values from 0 to 1023, as said below
- wavelet: float32 [4, 4], P('shot'), may hold values from -6 to 6
- receiver_index: int32 [4, 1024, 3], P('shot'), may hold values from 0 to 1023, as said below
- residual: float32 [4, 4, 1024], P('shot'), may hold values from -6 to 6
Outputs:
- final_wave: float32 [4, 1024, 64, 256], P('shot', 'dom')
- first_adjoint: float32 [4, 1024, 64, 256], P('shot', 'dom')
- gradient: float32 [1024, 64, 256], P('dom')
The draws below stay inside these ranges and needn't reach their ends.
Inputs may be any that keep to these rules, and one draw needn't show every extreme that they name: `source_index`: column 0 is a cell index along x below 1024, column 1 along z below 64, column 2 along y below 256. The first shot's source lies at the far corner of the grid and the second shot's source at depth 0. `receiver_index`: last index 0 is a cell index along x below 1024, 1 along z below 64, 2 along y below 256; receivers may share a cell. In every shot the first receiver lies at the far corner of the grid and the second at depth 0.
All inputs are finite; a program needn't handle non-finite values.
Results may differ from the reference program's by a relative error of at most 0.00002.
Values sent between devices are 32-bit elements; how exact they have to be, the bound alone decides.
A program may use at most 128 MiB of HBM per device.

```python
import math
import jax
import jax.numpy as jnp
from jax import lax

NZ = 64
NY = 256
RECS = 1024
STEPS = 4
REGIONS = 8
SHOTS = 4
NX = 1024


def draw_source_index(key, part):
    keys = jax.random.split(jax.random.fold_in(key, 11), 3)
    along_x = jax.random.randint(keys[0], (SHOTS,), 0, NX)
    along_z = jax.random.randint(keys[1], (SHOTS,), 0, NZ)
    along_y = jax.random.randint(keys[2], (SHOTS,), 0, NY)
    along_x = along_x.at[0].set(NX - 1)
    along_z = along_z.at[0].set(NZ - 1)
    along_y = along_y.at[0].set(NY - 1)
    along_z = along_z.at[1].set(0)
    return jnp.stack([along_x, along_z, along_y], axis=-1).astype(jnp.int32)


def draw_receiver_index(key, part):
    keys = jax.random.split(jax.random.fold_in(key, 23), 3)
    along_x = jax.random.randint(keys[0], (SHOTS, RECS), 0, NX)
    along_z = jax.random.randint(keys[1], (SHOTS, RECS), 0, NZ)
    along_y = jax.random.randint(keys[2], (SHOTS, RECS), 0, NY)
    along_x = along_x.at[:, 0].set(NX - 1)
    along_z = along_z.at[:, 0].set(NZ - 1)
    along_y = along_y.at[:, 0].set(NY - 1)
    along_z = along_z.at[:, 1].set(0)
    return jnp.stack([along_x, along_z, along_y], axis=-1).astype(jnp.int32)


def plant(values, key, smallest, top_value):
    dims = values.shape
    index_at = [jax.random.randint(jax.random.fold_in(key, axis), (), 0, dims[axis]) for axis in range(len(dims))]
    values = values.at[tuple(index_at)].set(smallest)
    longest = dims.index(max(dims))
    index_at[longest] = (index_at[longest] + 1) % dims[longest]
    return values.at[tuple(index_at)].set(top_value)


def shard_levels(rng, extent, shards, low, high):
    def one(dim, shards_of):
        heights = jax.random.uniform(jax.random.fold_in(jax.random.fold_in(rng, 6), dim), (shards_of,), jnp.float32, low / len(shards), high / len(shards))
        return jnp.repeat(jnp.exp(heights), extent[dim] // shards_of).reshape((-1,) + (1,) * (len(extent) - dim - 1))

    level = one(*shards[0])
    for cut in shards[1:]:
        level = level * one(*cut)
    return level


def scatter_about(key, dims, deviation, bound, cuts=(), dtype=jnp.bfloat16):
    entries = deviation * jax.random.normal(key, dims, jnp.float32)
    if cuts:
        entries = entries * shard_levels(key, dims, cuts, -0.22, 0.18)
    return jnp.clip(entries, -bound, bound).astype(dtype)


def setup_inputs(seed: int = 0) -> dict:
    seeds = jax.random.split(jax.random.key(seed), 11)
    wave_before = scatter_about(seeds[0], (SHOTS, NX, NZ, NY), 0.25, 1.5, ((0, 4), (1, 64)), jnp.float32)
    wave_current = scatter_about(seeds[1], (SHOTS, NX, NZ, NY), 0.25, 1.5, ((0, 4), (1, 64)), jnp.float32)
    adjoint_far = scatter_about(seeds[2], (SHOTS, NX, NZ, NY), 0.25, 1.5, ((0, 4), (1, 64)), jnp.float32)
    adjoint_near = scatter_about(seeds[3], (SHOTS, NX, NZ, NY), 0.25, 1.5, ((0, 4), (1, 64)), jnp.float32)
    labels = plant(jax.random.randint(seeds[4], (NX, NZ, NY), 0, REGIONS), jax.random.fold_in(seeds[4], 1), 0, REGIONS - 1).astype(jnp.int32)
    table = jnp.clip(jnp.exp(jax.random.uniform(seeds[5], (REGIONS,), jnp.float32, math.log(0.03), math.log(0.12))), 0.03, 0.12)
    source_index = draw_source_index(jax.random.fold_in(seeds[10], 71), 0)
    wavelet = scatter_about(seeds[7], (SHOTS, STEPS), 1.0, 6.0, ((0, 4),), jnp.float32)
    receiver_index = draw_receiver_index(jax.random.fold_in(seeds[10], 71), 0)
    residual = scatter_about(seeds[9], (SHOTS, STEPS, RECS), 1.0, 6.0, ((0, 4),), jnp.float32)
    return dict(wave_before=wave_before, wave_current=wave_current, adjoint_far=adjoint_far, adjoint_near=adjoint_near, labels=labels, table=table, source_index=source_index, wavelet=wavelet, receiver_index=receiver_index, residual=residual)


centre_coef = -205.0 / 72.0
side_coefs = (8.0 / 5.0, -1.0 / 5.0, 8.0 / 315.0, -1.0 / 560.0)


def laplace(field_in):
    size_x, size_z, size_y = field_in.shape
    padded = jnp.pad(field_in, 4)
    result = 3.0 * centre_coef * field_in
    for k in range(1, 5):
        coef = side_coefs[k - 1]
        result = result + coef * (
            padded[4 + k:4 + k + size_x, 4:4 + size_z, 4:4 + size_y]
            + padded[4 - k:4 - k + size_x, 4:4 + size_z, 4:4 + size_y]
            + padded[4:4 + size_x, 4 + k:4 + k + size_z, 4:4 + size_y]
            + padded[4:4 + size_x, 4 - k:4 - k + size_z, 4:4 + size_y]
            + padded[4:4 + size_x, 4:4 + size_z, 4 + k:4 + k + size_y]
            + padded[4:4 + size_x, 4:4 + size_z, 4 - k:4 - k + size_y])
    return result


def rates(labels, table):
    result = jnp.zeros(labels.shape, jnp.float32)
    for region in range(REGIONS):
        result = result + jnp.where(labels == region, table[region], jnp.zeros((), jnp.float32))
    return result


def one_shot(rate, items):
    wave_old, wave_now, far_field, near_field, source, wave_amps, receivers, traces = items
    previous, current = wave_old, wave_now
    stored = []
    for step in range(STEPS):
        lap_current = laplace(current)
        stored.append(lap_current)
        upcoming = 2.0 * current - previous + rate * lap_current
        upcoming = upcoming.at[source[0], source[1], source[2]].add(wave_amps[step])
        previous, current = current, upcoming
    later, adjoint = far_field, near_field
    gradient = jnp.zeros_like(rate)
    for step in reversed(range(STEPS)):
        gradient = gradient + adjoint * stored[step]
        earlier = 2.0 * adjoint - later + laplace(rate * adjoint)
        earlier = earlier.at[receivers[:, 0], receivers[:, 1], receivers[:, 2]].add(traces[step])
        later, adjoint = adjoint, earlier
    return current, adjoint, gradient


def reference(wave_before, wave_current, adjoint_far, adjoint_near, labels, table, source_index, wavelet, receiver_index, residual):
    rate = rates(labels, table)
    final_wave, first_adjoint, gradients = lax.map(
        lambda items: one_shot(rate, items),
        (wave_before, wave_current, adjoint_far, adjoint_near, source_index, wavelet, receiver_index, residual))
    return final_wave, first_adjoint, jnp.sum(gradients, axis=0)
```

```python
import functools

import jax
import jax.numpy as jnp
import numpy as np
from jax import lax
from jax.experimental import pallas as pl
from jax.experimental.pallas import tpu as pltpu
from jax.sharding import PartitionSpec as P

MESH = pl.DeviceIdType.MESH
F32 = jnp.float32
BF16 = jnp.bfloat16

scale = 5040.0
centre = 3.0 * -14350.0
sides = (8064.0, -1008.0, 128.0, -9.0)


def split(values):
    high = values.astype(BF16)
    rest = values - high.astype(F32)
    middle = rest.astype(BF16)
    low = (rest - middle.astype(F32)).astype(BF16)
    return high, middle, low


def band(rows, columns, block):
    row = lax.broadcasted_iota(jnp.int32, (rows, columns), 0)
    column = lax.broadcasted_iota(jnp.int32, (rows, columns), 1)
    away = jnp.abs(row - column)
    result = jnp.zeros((rows, columns), F32)
    for k in range(1, 5):
        result = jnp.where(away == k, sides[k - 1], result)
    if block:
        result = jnp.where(row // block == column // block, result, 0.0)
    return result.astype(BF16)


def kernel(
    doms,
    before_hbm, current_hbm, far_hbm, near_hbm, labels_hbm,
    table, source, wavelet, receivers, residual,
    final_hbm, first_hbm, gradient_hbm,
    ue, u0, u5, se, aa, lap, rate, labels, yzf, yza, stack, along_y, along_z,
    onehot, amounts, inject, spot, grad, near_grad, far_grad, partial, total,
    load_sem, store_sem, send_sem, recv_sem, gsend_sem, grecv_sem,
):
    shot = lax.axis_index("shot")
    dom = lax.axis_index("dom")
    planes, depth, across = u0.shape
    groups = planes // 4
    recs = receivers.shape[1]
    core = lax.rem(shot, 2)
    sibling = shot + 1 - 2 * core
    partner = lax.rem(shot + 2, 4)
    has_low = dom > 0
    has_high = dom < doms - 1

    barrier = pltpu.get_barrier_semaphore()

    def greet(device):
        pl.semaphore_signal(barrier, inc=1, device_id=device, device_id_type=MESH)

    greet({"shot": sibling})
    greet({"shot": partner})

    @pl.when(has_low)
    def _():
        greet({"dom": dom - 1})

    @pl.when(has_high)
    def _():
        greet({"dom": dom + 1})

    loads = [
        pltpu.make_async_copy(labels_hbm, labels, load_sem.at[0]),
        pltpu.make_async_copy(near_hbm.at[0], aa.at[1], load_sem.at[1]),
        pltpu.make_async_copy(current_hbm.at[0], ue.at[0, pl.ds(4, planes)], load_sem.at[2]),
        pltpu.make_async_copy(before_hbm.at[0], u0, load_sem.at[3]),
        pltpu.make_async_copy(far_hbm.at[0], aa.at[0], load_sem.at[4]),
    ]
    for load in loads:
        load.start()

    pl.semaphore_wait(barrier, 2 + jnp.where(has_low, 1, 0) + jnp.where(has_high, 1, 0))

    def to_low(e, source_ref):
        buffer = ue.at[e] if e < 4 else se.at[e - 4]
        return pltpu.make_async_remote_copy(
            source_ref, buffer.at[pl.ds(planes + 4, 4)], send_sem.at[0, e], recv_sem.at[0, e],
            device_id={"dom": dom - 1}, device_id_type=MESH,
        )

    def to_high(e, source_ref):
        buffer = ue.at[e] if e < 4 else se.at[e - 4]
        return pltpu.make_async_remote_copy(
            source_ref, buffer.at[pl.ds(0, 4)], send_sem.at[1, e], recv_sem.at[1, e],
            device_id={"dom": dom + 1}, device_id_type=MESH,
        )

    def low_edge(e):
        if e == 0:
            return current_hbm.at[0, pl.ds(0, 4)]
        return (ue.at[e] if e < 4 else se.at[e - 4]).at[pl.ds(4, 4)]

    def high_edge(e):
        if e == 0:
            return current_hbm.at[0, pl.ds(planes - 4, 4)]
        return (ue.at[e] if e < 4 else se.at[e - 4]).at[pl.ds(planes, 4)]

    def send_low(e):
        @pl.when(has_low)
        def _():
            to_low(e, low_edge(e)).start()

    def send_high(e):
        @pl.when(has_high)
        def _():
            to_high(e, high_edge(e)).start()

    def wait_low(e):
        @pl.when(has_low)
        def _():
            to_high(e, high_edge(e)).wait_recv()

    def wait_high(e):
        @pl.when(has_high)
        def _():
            to_low(e, low_edge(e)).wait_recv()

    send_low(0)
    send_high(0)

    @pl.when(dom == 0)
    def _():
        for e in range(4):
            ue[e, 0:4] = jnp.zeros((4, depth, across), F32)
            se[e, 0:4] = jnp.zeros((4, depth, across), F32)

    @pl.when(dom == doms - 1)
    def _():
        for e in range(4):
            ue[e, planes + 4:planes + 8] = jnp.zeros((4, depth, across), F32)
            se[e, planes + 4:planes + 8] = jnp.zeros((4, depth, across), F32)

    speeds = [table[k] * (1.0 / scale) for k in range(table.shape[0])]
    loads[0].wait()
    loads[1].wait()

    def first_plane(p):
        def rows(i, _):
            r = pl.ds(pl.multiple_of(i * 16, 16), 16)
            region = labels[p, r, :]
            speed = jnp.full(region.shape, speeds[0], F32)
            for k in range(1, len(speeds)):
                speed = jnp.where(region == k, speeds[k], speed)
            rate[p, r, :] = speed
            se[0, p + 4, r, :] = speed * aa[1, p, r, :]
            return 0

        lax.fori_loop(0, depth // 16, rows, 0)

    def first_group(base):
        lax.fori_loop(0, 4, lambda j, c: (first_plane(base + j), c)[1], 0)

    first_group(0)
    send_low(4)
    first_group(planes - 4)
    send_high(4)
    lax.fori_loop(4, planes - 4, lambda p, c: (first_plane(p), c)[1], 0)

    along_y[...] = band(across, across, 0)
    plane_band = band(4 * depth, 4 * depth, depth)
    for k in range(3):
        along_z[:, k * 4 * depth:(k + 1) * 4 * depth] = plane_band

    row = lax.broadcasted_iota(jnp.int32, (depth, across), 0)
    column = lax.broadcasted_iota(jnp.int32, (depth, across), 1)
    spot[...] = jnp.where((row == source[0, 1]) & (column == source[0, 2]), 1.0, 0.0).astype(F32)
    source_plane = source[0, 0] - dom * planes

    def across_stage(ext, out):
        def group(g, _):
            for q in range(4):
                def rows(i, _, q=q):
                    at = pl.multiple_of(i * 16, 16)
                    parts = split(ext[4 + 4 * g + q, pl.ds(at, 16), :])
                    for k in range(3):
                        stack[pl.ds(pl.multiple_of(at + (4 * k + q) * depth, 16), 16), :] = parts[k]
                    return 0

                lax.fori_loop(0, depth // 16, rows, 0, unroll=True)
            size = 4 * depth
            in_y = jnp.dot(stack[...], along_y[...], preferred_element_type=F32)
            in_z = jnp.dot(along_z[...], stack[...], preferred_element_type=F32)
            both = (in_y[2 * size:] + in_y[size:2 * size]) + in_y[:size] + in_z
            out[pl.ds(4 * g, 4)] = both.reshape(4, depth, across)
            return 0

        lax.fori_loop(0, groups, group, 0)

    def laplace(planes_of, j, rest):
        result = rest + centre * planes_of[j + 4]
        for k in range(1, 5):
            result = result + sides[k - 1] * (planes_of[j + 4 + k] + planes_of[j + 4 - k])
        return result

    def forward_group(n, g):
        pulses = [jnp.where(source_plane == 4 * g + j, wavelet[0, n], 0.0) for j in range(4)]

        def rows(i, _):
            r = pl.ds(pl.multiple_of(i * 8, 8), 8)
            window = [ue[n, 4 * g + q, r, :] for q in range(12)]
            for j in range(4):
                p = 4 * g + j
                curve = laplace(window, j, yzf[p, r, :])
                lap[n, p, r, :] = curve
                previous = u0[p, r, :] if n == 0 else ue[n - 1, p + 4, r, :]
                upcoming = 2.0 * window[j + 4] - previous + rate[p, r, :] * curve
                upcoming = upcoming + pulses[j] * spot[r, :]
                if n == 3:
                    u5[p, r, :] = upcoming
                else:
                    ue[n + 1, p + 4, r, :] = upcoming
            return 0

        lax.fori_loop(0, depth // 8, rows, 0)

    def adjoint_group(m, g):
        def rows(i, _):
            r = pl.ds(pl.multiple_of(i * 8, 8), 8)
            window = [se[m, 4 * g + q, r, :] for q in range(12)]
            for j in range(4):
                p = 4 * g + j
                curve = laplace(window, j, yza[p, r, :])
                earlier = 2.0 * aa[m + 1, p, r, :] - aa[m, p, r, :] + curve + inject[3 - m, p, r, :]
                aa[m + 2, p, r, :] = earlier
                if m < 3:
                    se[m + 1, p + 4, r, :] = rate[p, r, :] * earlier
            return 0

        lax.fori_loop(0, depth // 8, rows, 0)

    def middle(one, n):
        lax.fori_loop(1, groups - 1, lambda g, c: (one(n, g), c)[1], 0)

    cell = (receivers[0:1, :] - dom * planes) * depth + receivers[1:2, :]

    def onehot_rows(i, _):
        at = pl.multiple_of(i * 16, 16)
        here = lax.broadcasted_iota(jnp.int32, (16, recs), 0) + at
        onehot[pl.ds(at, 16), :] = jnp.where(here == cell, 1.0, 0.0).astype(BF16)
        return 0

    def inject_step(n, _):
        value = residual[pl.ds(n, 1), :]
        parts = [part.astype(F32) for part in split(value)]

        def columns(i, _):
            at = pl.multiple_of(i * 16, 16)
            here = lax.broadcasted_iota(jnp.int32, (16, recs), 0) + at == receivers[2:3, :]
            for k in range(3):
                amounts[pl.ds(pl.multiple_of(at + k * across, 16), 16), :] = jnp.where(here, parts[k], 0.0).astype(BF16)
            return 0

        lax.fori_loop(0, across // 16, columns, 0)

        def group(g, _):
            rows = pl.ds(pl.multiple_of(g * 4 * depth, 4 * depth), 4 * depth)
            spread = lax.dot_general(
                onehot[rows, :], amounts[...], (((1,), (1,)), ((), ())), preferred_element_type=F32
            )
            both = (spread[:, 2 * across:] + spread[:, across:2 * across]) + spread[:, :across]
            inject[n, pl.ds(4 * g, 4)] = both.reshape(4, depth, across)
            return 0

        lax.fori_loop(0, groups, group, 0)
        return 0

    def combine(p, _):
        def rows(i, _):
            r = pl.ds(pl.multiple_of(i * 16, 16), 16)
            value = aa[1, p, r, :] * lap[3, p, r, :]
            for n in (2, 1, 0):
                value = value + aa[4 - n, p, r, :] * lap[n, p, r, :]
            grad[p, r, :] = value
            return 0

        lax.fori_loop(0, depth // 16, rows, 0)
        return 0

    mine = (4 + 4 * core, (planes - 4) * core)
    other = (8 - 4 * core, (planes - 4) * (1 - core))

    def to_sibling(c):
        return pltpu.make_async_remote_copy(
            grad.at[pl.ds(other[c], 4)], near_grad.at[c], gsend_sem.at[0, c], grecv_sem.at[0, c],
            device_id={"shot": sibling}, device_id_type=MESH,
        )

    def to_partner(c):
        return pltpu.make_async_remote_copy(
            partial.at[c], far_grad.at[c], gsend_sem.at[1, c], grecv_sem.at[1, c],
            device_id={"shot": partner}, device_id_type=MESH,
        )

    def total_to_sibling(c):
        return pltpu.make_async_remote_copy(
            total.at[c], gradient_hbm.at[pl.ds(mine[c], 4)], gsend_sem.at[2, c], grecv_sem.at[2, c],
            device_id={"shot": sibling}, device_id_type=MESH,
        )

    def total_home(c):
        return pltpu.make_async_copy(total.at[c], gradient_hbm.at[pl.ds(mine[c], 4)], store_sem.at[c])

    def sum_near(c):
        to_sibling(c).wait_recv()

        def one(j, _):
            partial[c, j] = grad[mine[c] + j] + near_grad[c, j]
            return 0

        lax.fori_loop(0, 4, one, 0)
        to_partner(c).start()

    def sum_far(c):
        to_partner(c).wait_recv()

        def one(j, _):
            total[c, j] = (partial[c, j] + far_grad[c, j]) * (1.0 / scale)
            return 0

        lax.fori_loop(0, 4, one, 0)
        total_to_sibling(c).start()
        total_home(c).start()

    loads[2].wait()
    across_stage(ue.at[0], yzf)
    loads[3].wait()
    middle(forward_group, 0)
    lax.fori_loop(0, planes * depth // 16, onehot_rows, 0)
    lax.fori_loop(3, 4, inject_step, 0)

    stores = [
        pltpu.make_async_copy(u5, final_hbm.at[0], store_sem.at[2]),
        pltpu.make_async_copy(aa.at[5], first_hbm.at[0], store_sem.at[3]),
    ]

    for n in range(4):
        wait_low(n)
        forward_group(n, 0)
        if n < 3:
            send_low(n + 1)
        wait_high(n)
        forward_group(n, groups - 1)
        if n < 3:
            send_high(n + 1)
            across_stage(ue.at[n + 1], yzf)
            middle(forward_group, n + 1)
        if n == 0:
            loads[4].wait()
            across_stage(se.at[0], yza)
            middle(adjoint_group, 0)
        if n == 2:
            lax.fori_loop(4, planes - 4, combine, 0)
            to_sibling(0).start()
        if n == 3:
            lax.fori_loop(0, 4, combine, 0)
            lax.fori_loop(planes - 4, planes, combine, 0)
            to_sibling(1).start()
            stores[0].start()
            sum_far(0)
            sum_near(1)
        wait_low(n + 4)
        adjoint_group(n, 0)
        if n < 3:
            send_low(n + 5)
        wait_high(n + 4)
        adjoint_group(n, groups - 1)
        if n < 3:
            send_high(n + 5)
        if n == 2:
            sum_near(0)
        if n == 0:
            lax.fori_loop(0, 3, inject_step, 0)
        if n < 3:
            across_stage(se.at[n + 1], yza)
            middle(adjoint_group, n + 1)
    stores[1].start()
    sum_far(1)

    for c in range(2):
        total_to_sibling(c).wait_recv()
    for e in range(8):
        @pl.when(has_low)
        def _():
            to_low(e, low_edge(e)).wait_send()

        @pl.when(has_high)
        def _():
            to_high(e, high_edge(e)).wait_send()
    for c in range(2):
        to_sibling(c).wait_send()
        to_partner(c).wait_send()
        total_to_sibling(c).wait_send()
        total_home(c).wait()
    for store in stores:
        store.wait()


def per_device(
    doms, wave_before, wave_current, adjoint_far, adjoint_near, labels, table,
    source_index, wavelet, receiver_index, residual,
):
    block = wave_current.shape
    planes, depth, across = labels.shape
    recs = receiver_index.shape[1]
    field = (planes, depth, across)
    extended = (4, planes + 8, depth, across)
    whole = pl.BlockSpec(memory_space=pl.ANY)
    scalars = pl.BlockSpec(memory_space=pltpu.SMEM)
    vectors = pl.BlockSpec(memory_space=pltpu.VMEM)
    return pl.pallas_call(
        functools.partial(kernel, doms),
        out_shape=(
            jax.ShapeDtypeStruct(block, F32),
            jax.ShapeDtypeStruct(block, F32),
            jax.ShapeDtypeStruct(field, F32),
        ),
        in_specs=[whole] * 5 + [scalars] * 3 + [vectors] * 2,
        out_specs=(whole, whole, whole),
        scratch_shapes=[
            pltpu.VMEM(extended, F32),
            pltpu.VMEM(field, F32),
            pltpu.VMEM(field, F32),
            pltpu.VMEM(extended, F32),
            pltpu.VMEM((6,) + field, F32),
            pltpu.VMEM((4,) + field, F32),
            pltpu.VMEM(field, F32),
            pltpu.VMEM(field, jnp.int32),
            pltpu.VMEM(field, F32),
            pltpu.VMEM(field, F32),
            pltpu.VMEM((12 * depth, across), BF16),
            pltpu.VMEM((across, across), BF16),
            pltpu.VMEM((4 * depth, 12 * depth), BF16),
            pltpu.VMEM((planes * depth, recs), BF16),
            pltpu.VMEM((3 * across, recs), BF16),
            pltpu.VMEM((4,) + field, F32),
            pltpu.VMEM((depth, across), F32),
            pltpu.VMEM(field, F32),
            pltpu.VMEM((2, 4, depth, across), F32),
            pltpu.VMEM((2, 4, depth, across), F32),
            pltpu.VMEM((2, 4, depth, across), F32),
            pltpu.VMEM((2, 4, depth, across), F32),
            pltpu.SemaphoreType.DMA((5,)),
            pltpu.SemaphoreType.DMA((4,)),
            pltpu.SemaphoreType.DMA((2, 8)),
            pltpu.SemaphoreType.DMA((2, 8)),
            pltpu.SemaphoreType.DMA((3, 2)),
            pltpu.SemaphoreType.DMA((3, 2)),
        ],
        compiler_params=pltpu.CompilerParams(
            collective_id=0, has_side_effects=True, vmem_limit_bytes=56 << 20
        ),
        name="window",
    )(
        wave_before, wave_current, adjoint_far, adjoint_near, labels, table,
        source_index, wavelet, jnp.transpose(receiver_index[0]), residual[0],
    )


def solution(mesh):
    fields = P("shot", "dom", None, None)
    return jax.shard_map(
        functools.partial(per_device, mesh.shape["dom"]),
        mesh=mesh,
        in_specs=(
            fields, fields, fields, fields, P("dom", None, None), P(),
            P("shot", None), P("shot", None), P("shot", None, None), P("shot", None, None),
        ),
        out_specs=(fields, fields, P("dom", None, None)),
        check_vma=False,
    )
```

```python
import functools

import jax
import jax.numpy as jnp
import numpy as np
from jax import lax
from jax.experimental import pallas as pl
from jax.experimental.pallas import tpu as pltpu
from jax.sharding import PartitionSpec as P

MESH = pl.DeviceIdType.MESH
F32 = jnp.float32
BF16 = jnp.bfloat16

ring = 8

scale = 5040.0
centre = 3.0 * -14350.0
sides = (8064.0, -1008.0, 128.0, -9.0)


def split(values):
    high = values.astype(BF16)
    rest = values - high.astype(F32)
    middle = rest.astype(BF16)
    low = (rest - middle.astype(F32)).astype(BF16)
    return high, middle, low


def band(rows, columns, block):
    row = lax.broadcasted_iota(jnp.int32, (rows, columns), 0)
    column = lax.broadcasted_iota(jnp.int32, (rows, columns), 1)
    away = jnp.abs(row - column)
    result = jnp.zeros((rows, columns), F32)
    for k in range(1, 5):
        result = jnp.where(away == k, sides[k - 1], result)
    if block:
        result = jnp.where(row // block == column // block, result, 0.0)
    return result.astype(BF16)


def kernel(
    doms,
    before_hbm, current_hbm, far_hbm, near_hbm, labels_hbm,
    table, source, wavelet, receivers, residual,
    final, first, gradient,
    ue, u0, se, aa, lap, rate, labels, yzf, yza, stack, along_y, along_z,
    onehot, amounts, inject, spot, grad, near_grad, far_grad, partial, passing,
    load_sem, send_sem, recv_sem, gsend_sem, grecv_sem, psend_sem, precv_sem,
):
    shot = lax.axis_index("shot")
    dom = lax.axis_index("dom")
    planes, depth, across = u0.shape
    groups = planes // 4
    recs = receivers.shape[2]
    core = lax.rem(shot, 2)
    sibling = shot + 1 - 2 * core
    partner = lax.rem(shot + 2, 4)
    place = lax.rem(dom, ring)
    at_end = (place == 0) | (place == ring - 1)
    passes = (place == 1) | (place == ring - 2)
    inside = jnp.where(place == 0, dom + 1, dom - 1)
    outside = jnp.where(place == 1, dom - 1, dom + 1)
    has_low = dom > 0
    has_high = dom < doms - 1

    barrier = pltpu.get_barrier_semaphore()

    def greet(device):
        pl.semaphore_signal(barrier, inc=1, device_id=device, device_id_type=MESH)

    greet({"shot": sibling})
    greet({"shot": partner})

    @pl.when(at_end)
    def _():
        greet({"shot": partner, "dom": inside})

    @pl.when(passes)
    def _():
        greet({"shot": partner, "dom": outside})

    @pl.when(has_low)
    def _():
        greet({"dom": dom - 1})

    @pl.when(has_high)
    def _():
        greet({"dom": dom + 1})

    loads = [
        pltpu.make_async_copy(labels_hbm, labels, load_sem.at[0]),
        pltpu.make_async_copy(near_hbm.at[0], aa.at[1], load_sem.at[1]),
        pltpu.make_async_copy(current_hbm.at[0], ue.at[0, pl.ds(4, planes)], load_sem.at[2]),
        pltpu.make_async_copy(before_hbm.at[0], u0, load_sem.at[3]),
        pltpu.make_async_copy(far_hbm.at[0], aa.at[0], load_sem.at[4]),
    ]
    for load in loads:
        load.start()

    peers = 2 + jnp.where(at_end | passes, 1, 0) + jnp.where(has_low, 1, 0) + jnp.where(has_high, 1, 0)
    pl.semaphore_wait(barrier, peers)

    def to_low(e, source_ref):
        buffer = ue.at[e] if e < 4 else se.at[e - 4]
        return pltpu.make_async_remote_copy(
            source_ref, buffer.at[pl.ds(planes + 4, 4)], send_sem.at[0, e], recv_sem.at[0, e],
            device_id={"dom": dom - 1}, device_id_type=MESH,
        )

    def to_high(e, source_ref):
        buffer = ue.at[e] if e < 4 else se.at[e - 4]
        return pltpu.make_async_remote_copy(
            source_ref, buffer.at[pl.ds(0, 4)], send_sem.at[1, e], recv_sem.at[1, e],
            device_id={"dom": dom + 1}, device_id_type=MESH,
        )

    def low_edge(e):
        if e == 0:
            return current_hbm.at[0, pl.ds(0, 4)]
        return (ue.at[e] if e < 4 else se.at[e - 4]).at[pl.ds(4, 4)]

    def high_edge(e):
        if e == 0:
            return current_hbm.at[0, pl.ds(planes - 4, 4)]
        return (ue.at[e] if e < 4 else se.at[e - 4]).at[pl.ds(planes, 4)]

    def send_low(e):
        @pl.when(has_low)
        def _():
            to_low(e, low_edge(e)).start()

    def send_high(e):
        @pl.when(has_high)
        def _():
            to_high(e, high_edge(e)).start()

    def wait_low(e):
        @pl.when(has_low)
        def _():
            to_high(e, high_edge(e)).wait_recv()

    def wait_high(e):
        @pl.when(has_high)
        def _():
            to_low(e, low_edge(e)).wait_recv()

    send_low(0)
    send_high(0)

    @pl.when(dom == 0)
    def _():
        for e in range(4):
            ue[e, 0:4] = jnp.zeros((4, depth, across), F32)
            se[e, 0:4] = jnp.zeros((4, depth, across), F32)

    @pl.when(dom == doms - 1)
    def _():
        for e in range(4):
            ue[e, planes + 4:planes + 8] = jnp.zeros((4, depth, across), F32)
            se[e, planes + 4:planes + 8] = jnp.zeros((4, depth, across), F32)

    speeds = [table[k] * (1.0 / scale) for k in range(table.shape[0])]
    loads[0].wait()
    loads[1].wait()

    def first_plane(p):
        def rows(i, _):
            r = pl.ds(pl.multiple_of(i * 16, 16), 16)
            region = labels[p, r, :]
            speed = jnp.full(region.shape, speeds[0], F32)
            for k in range(1, len(speeds)):
                speed = jnp.where(region == k, speeds[k], speed)
            rate[p, r, :] = speed
            se[0, p + 4, r, :] = speed * aa[1, p, r, :]
            return 0

        lax.fori_loop(0, depth // 16, rows, 0)

    def first_group(base):
        lax.fori_loop(0, 4, lambda j, c: (first_plane(base + j), c)[1], 0)

    first_group(0)
    send_low(4)
    first_group(planes - 4)
    send_high(4)
    lax.fori_loop(4, planes - 4, lambda p, c: (first_plane(p), c)[1], 0)

    along_y[...] = band(across, across, 0)
    plane_band = band(4 * depth, 4 * depth, depth)
    for k in range(3):
        along_z[:, k * 4 * depth:(k + 1) * 4 * depth] = plane_band

    row = lax.broadcasted_iota(jnp.int32, (depth, across), 0)
    column = lax.broadcasted_iota(jnp.int32, (depth, across), 1)
    spot[...] = jnp.where((row == source[0, 1]) & (column == source[0, 2]), 1.0, 0.0).astype(F32)
    source_plane = source[0, 0] - dom * planes

    def across_stage(ext, out):
        def group(g, _):
            for q in range(4):
                def rows(i, _, q=q):
                    at = pl.multiple_of(i * 16, 16)
                    parts = split(ext[4 + 4 * g + q, pl.ds(at, 16), :])
                    for k in range(3):
                        stack[pl.ds(pl.multiple_of(at + (4 * k + q) * depth, 16), 16), :] = parts[k]
                    return 0

                lax.fori_loop(0, depth // 16, rows, 0, unroll=True)
            size = 4 * depth
            in_y = jnp.dot(stack[...], along_y[...], preferred_element_type=F32)
            in_z = jnp.dot(along_z[...], stack[...], preferred_element_type=F32)
            both = (in_y[2 * size:] + in_y[size:2 * size]) + in_y[:size] + in_z
            out[pl.ds(4 * g, 4)] = both.reshape(4, depth, across)
            return 0

        lax.fori_loop(0, groups, group, 0)

    def laplace(planes_of, j, rest):
        result = rest + centre * planes_of[j + 4]
        for k in range(1, 5):
            result = result + sides[k - 1] * (planes_of[j + 4 + k] + planes_of[j + 4 - k])
        return result

    def forward_group(n, g):
        pulses = [jnp.where(source_plane == 4 * g + j, wavelet[0, n], 0.0) for j in range(4)]

        def rows(i, _):
            r = pl.ds(pl.multiple_of(i * 8, 8), 8)
            window = [ue[n, 4 * g + q, r, :] for q in range(12)]
            for j in range(4):
                p = 4 * g + j
                curve = laplace(window, j, yzf[p, r, :])
                lap[n, p, r, :] = curve
                previous = u0[p, r, :] if n == 0 else ue[n - 1, p + 4, r, :]
                upcoming = 2.0 * window[j + 4] - previous + rate[p, r, :] * curve
                upcoming = upcoming + pulses[j] * spot[r, :]
                if n == 3:
                    final[0, p, r, :] = upcoming
                else:
                    ue[n + 1, p + 4, r, :] = upcoming
            return 0

        lax.fori_loop(0, depth // 8, rows, 0)

    def adjoint_group(m, g):
        def rows(i, _):
            r = pl.ds(pl.multiple_of(i * 8, 8), 8)
            window = [se[m, 4 * g + q, r, :] for q in range(12)]
            for j in range(4):
                p = 4 * g + j
                curve = laplace(window, j, yza[p, r, :])
                earlier = 2.0 * aa[m + 1, p, r, :] - aa[m, p, r, :] + curve + inject[3 - m, p, r, :]
                if m == 3:
                    first[0, p, r, :] = earlier
                else:
                    aa[m + 2, p, r, :] = earlier
                    se[m + 1, p + 4, r, :] = rate[p, r, :] * earlier
            return 0

        lax.fori_loop(0, depth // 8, rows, 0)

    def middle(one, n):
        lax.fori_loop(1, groups - 1, lambda g, c: (one(n, g), c)[1], 0)

    cell = (receivers[0] - dom * planes) * depth + receivers[1]

    def onehot_rows(i, _):
        at = pl.multiple_of(i * 16, 16)
        here = lax.broadcasted_iota(jnp.int32, (16, recs), 0) + at
        onehot[pl.ds(at, 16), :] = jnp.where(here == cell, 1.0, 0.0).astype(BF16)
        return 0

    lax.fori_loop(0, planes * depth // 16, onehot_rows, 0)

    def inject_step(n, _):
        value = residual[pl.ds(n, 1), :]
        parts = [part.astype(F32) for part in split(value)]

        def columns(i, _):
            at = pl.multiple_of(i * 16, 16)
            here = lax.broadcasted_iota(jnp.int32, (16, recs), 0) + at == receivers[2]
            for k in range(3):
                amounts[pl.ds(pl.multiple_of(at + k * across, 16), 16), :] = jnp.where(here, parts[k], 0.0).astype(BF16)
            return 0

        lax.fori_loop(0, across // 16, columns, 0)

        def group(g, _):
            rows = pl.ds(pl.multiple_of(g * 4 * depth, 4 * depth), 4 * depth)
            spread = lax.dot_general(
                onehot[rows, :], amounts[...], (((1,), (1,)), ((), ())), preferred_element_type=F32
            )
            both = (spread[:, 2 * across:] + spread[:, across:2 * across]) + spread[:, :across]
            inject[n, pl.ds(4 * g, 4)] = both.reshape(4, depth, across)
            return 0

        lax.fori_loop(0, groups, group, 0)
        return 0

    def combine(p, _):
        def rows(i, _):
            r = pl.ds(pl.multiple_of(i * 16, 16), 16)
            value = aa[1, p, r, :] * lap[3, p, r, :]
            for n in (2, 1, 0):
                value = value + aa[4 - n, p, r, :] * lap[n, p, r, :]
            grad[p, r, :] = value
            return 0

        lax.fori_loop(0, depth // 16, rows, 0)
        return 0

    mine = (4 + 4 * core, (planes - 4) * core)
    other = (8 - 4 * core, (planes - 4) * (1 - core))

    def to_sibling(c):
        return pltpu.make_async_remote_copy(
            grad.at[pl.ds(other[c], 4)], near_grad.at[c], gsend_sem.at[0, c], grecv_sem.at[0, c],
            device_id={"shot": sibling}, device_id_type=MESH,
        )

    def to_partner(c):
        return pltpu.make_async_remote_copy(
            partial.at[c], far_grad.at[c], gsend_sem.at[1, c], grecv_sem.at[1, c],
            device_id={"shot": partner}, device_id_type=MESH,
        )

    def to_passer():
        return pltpu.make_async_remote_copy(
            partial.at[0], passing, psend_sem.at[0], precv_sem.at[0],
            device_id={"shot": partner, "dom": inside}, device_id_type=MESH,
        )

    def pass_on():
        return pltpu.make_async_remote_copy(
            passing, far_grad.at[0], psend_sem.at[1], precv_sem.at[1],
            device_id={"dom": outside}, device_id_type=MESH,
        )

    def total_to_sibling(c):
        return pltpu.make_async_remote_copy(
            gradient.at[pl.ds(mine[c], 4)], gradient.at[pl.ds(mine[c], 4)], gsend_sem.at[2, c], grecv_sem.at[2, c],
            device_id={"shot": sibling}, device_id_type=MESH,
        )

    def sum_near(c):
        to_sibling(c).wait_recv()

        def one(j, _):
            partial[c, j] = grad[mine[c] + j] + near_grad[c, j]
            return 0

        lax.fori_loop(0, 4, one, 0)
        if c == 1:
            to_partner(c).start()
        else:
            @pl.when(at_end)
            def _():
                to_passer().start()

            @pl.when(jnp.logical_not(at_end))
            def _():
                to_partner(c).start()

    def sum_far(c):
        if c == 1:
            to_partner(c).wait_recv()
        else:
            @pl.when(at_end)
            def _():
                pass_on().wait_recv()

            @pl.when(jnp.logical_not(at_end))
            def _():
                to_partner(c).wait_recv()

        def one(j, _):
            gradient[mine[c] + j] = (partial[c, j] + far_grad[c, j]) * (1.0 / scale)
            return 0

        lax.fori_loop(0, 4, one, 0)
        total_to_sibling(c).start()

    loads[2].wait()
    across_stage(ue.at[0], yzf)
    loads[3].wait()
    middle(forward_group, 0)

    for n in range(4):
        wait_low(n)
        forward_group(n, 0)
        if n < 3:
            send_low(n + 1)
        wait_high(n)
        forward_group(n, groups - 1)
        if n < 3:
            send_high(n + 1)
            across_stage(ue.at[n + 1], yzf)
            middle(forward_group, n + 1)
        if n == 0:
            loads[4].wait()
            lax.fori_loop(3, 4, inject_step, 0)
            across_stage(se.at[0], yza)
            middle(adjoint_group, 0)
        if n == 2:
            lax.fori_loop(4, planes - 4, combine, 0)
            to_sibling(0).start()
            sum_near(0)
        if n == 3:
            lax.fori_loop(0, 4, combine, 0)
            lax.fori_loop(planes - 4, planes, combine, 0)
            to_sibling(1).start()

            @pl.when(passes)
            def _():
                to_passer().wait_recv()
                pass_on().start()

            sum_near(1)
        if n == 1:
            lax.fori_loop(1, 2, inject_step, 0)
        wait_low(n + 4)
        adjoint_group(n, 0)
        if n < 3:
            send_low(n + 5)
        wait_high(n + 4)
        adjoint_group(n, groups - 1)
        if n < 3:
            send_high(n + 5)
        if n < 2:
            lax.fori_loop(2 - 2 * n, 3 - 2 * n, inject_step, 0)
        if n < 3:
            across_stage(se.at[n + 1], yza)
            middle(adjoint_group, n + 1)
    sum_far(0)
    sum_far(1)

    for c in range(2):
        total_to_sibling(c).wait_recv()
    for e in range(8):
        @pl.when(has_low)
        def _():
            to_low(e, low_edge(e)).wait_send()

        @pl.when(has_high)
        def _():
            to_high(e, high_edge(e)).wait_send()
    for c in range(2):
        to_sibling(c).wait_send()
        total_to_sibling(c).wait_send()

    @pl.when(at_end)
    def _():
        to_passer().wait_send()

    @pl.when(passes)
    def _():
        pass_on().wait_send()

    @pl.when(jnp.logical_not(at_end))
    def _():
        to_partner(0).wait_send()

    to_partner(1).wait_send()


def per_device(
    doms, wave_before, wave_current, adjoint_far, adjoint_near, labels, table,
    source_index, wavelet, receiver_index, residual,
):
    block = wave_current.shape
    planes, depth, across = labels.shape
    recs = receiver_index.shape[1]
    field = (planes, depth, across)
    extended = (4, planes + 8, depth, across)
    whole = pl.BlockSpec(memory_space=pltpu.HBM)
    scalars = pl.BlockSpec(memory_space=pltpu.SMEM)
    vectors = pl.BlockSpec(memory_space=pltpu.VMEM)
    return pl.pallas_call(
        functools.partial(kernel, doms),
        out_shape=(
            pltpu.VMEM(block, F32),
            pltpu.VMEM(block, F32),
            pltpu.VMEM(field, F32),
        ),
        in_specs=[whole] * 5 + [scalars] * 3 + [vectors] * 2,
        out_specs=(vectors, vectors, vectors),
        scratch_shapes=[
            pltpu.VMEM(extended, F32),
            pltpu.VMEM(field, F32),
            pltpu.VMEM(extended, F32),
            pltpu.VMEM((5,) + field, F32),
            pltpu.VMEM((4,) + field, F32),
            pltpu.VMEM(field, F32),
            pltpu.VMEM(field, jnp.int32),
            pltpu.VMEM(field, F32),
            pltpu.VMEM(field, F32),
            pltpu.VMEM((12 * depth, across), BF16),
            pltpu.VMEM((across, across), BF16),
            pltpu.VMEM((4 * depth, 12 * depth), BF16),
            pltpu.VMEM((planes * depth, recs), BF16),
            pltpu.VMEM((3 * across, recs), BF16),
            pltpu.VMEM((4,) + field, F32),
            pltpu.VMEM((depth, across), F32),
            pltpu.VMEM(field, F32),
            pltpu.VMEM((2, 4, depth, across), F32),
            pltpu.VMEM((2, 4, depth, across), F32),
            pltpu.VMEM((2, 4, depth, across), F32),
            pltpu.VMEM((4, depth, across), F32),
            pltpu.SemaphoreType.DMA((5,)),
            pltpu.SemaphoreType.DMA((2, 8)),
            pltpu.SemaphoreType.DMA((2, 8)),
            pltpu.SemaphoreType.DMA((3, 2)),
            pltpu.SemaphoreType.DMA((3, 2)),
            pltpu.SemaphoreType.DMA((2,)),
            pltpu.SemaphoreType.DMA((2,)),
        ],
        compiler_params=pltpu.CompilerParams(
            collective_id=0, has_side_effects=True, vmem_limit_bytes=60 << 20
        ),
        name="window",
    )(
        wave_before, wave_current, adjoint_far, adjoint_near, labels, table,
        source_index, wavelet, jnp.transpose(receiver_index, (2, 0, 1)), residual[0],
    )


def solution(mesh):
    fields = P("shot", "dom", None, None)
    return jax.shard_map(
        functools.partial(per_device, mesh.shape["dom"]),
        mesh=mesh,
        in_specs=(
            fields, fields, fields, fields, P("dom", None, None), P(),
            P("shot", None), P("shot", None), P("shot", None, None), P("shot", None, None),
        ),
        out_specs=(fields, fields, P("dom", None, None)),
        check_vma=False,
    )
```

```python
import functools

import jax
import jax.numpy as jnp
import numpy as np
from jax import lax
from jax.experimental import pallas as pl
from jax.experimental.pallas import tpu as pltpu
from jax.sharding import PartitionSpec as P

MESH = pl.DeviceIdType.MESH
F32 = jnp.float32
BF16 = jnp.bfloat16

ring = 8

scale = 5040.0
centre = 3.0 * -14350.0
sides = (8064.0, -1008.0, 128.0, -9.0)


def split(values):
    high = values.astype(BF16)
    rest = values - high.astype(F32)
    middle = rest.astype(BF16)
    low = (rest - middle.astype(F32)).astype(BF16)
    return high, middle, low


def band(rows, columns, block):
    row = lax.broadcasted_iota(jnp.int32, (rows, columns), 0)
    column = lax.broadcasted_iota(jnp.int32, (rows, columns), 1)
    away = jnp.abs(row - column)
    result = jnp.zeros((rows, columns), F32)
    for k in range(1, 5):
        result = jnp.where(away == k, sides[k - 1], result)
    if block:
        result = jnp.where(row // block == column // block, result, 0.0)
    return result.astype(BF16)


def kernel(
    doms,
    before_hbm, current_hbm, far_hbm, near_hbm, labels_hbm,
    table_hbm, source_hbm, wavelet_hbm, receivers_hbm, residual_hbm,
    final, first, gradient,
    table, source, wavelet, receivers, residual, ue, u0, se, aa, lap, rate, labels, yzf, yza, stack, along_y, along_z,
    onehot, amounts, inject, spot, grad, near_grad, far_grad, partial, passing,
    load_sem, send_sem, recv_sem, gsend_sem, grecv_sem,
):
    shot = lax.axis_index("shot")
    dom = lax.axis_index("dom")
    planes, depth, across = u0.shape
    groups = planes // 4
    recs = receivers.shape[2]
    core = lax.rem(shot, 2)
    sibling = shot + 1 - 2 * core
    partner = lax.rem(shot + 2, 4)
    place = lax.rem(dom, ring)
    at_end = (place == 0) | (place == ring - 1)
    passes = (place == 1) | (place == ring - 2)
    inside = jnp.where(place == 0, dom + 1, dom - 1)
    outside = jnp.where(place == 1, dom - 1, dom + 1)
    has_low = dom > 0
    has_high = dom < doms - 1

    barrier = pltpu.get_barrier_semaphore()

    def greet(device):
        pl.semaphore_signal(barrier, inc=1, device_id=device, device_id_type=MESH)

    greet({"shot": sibling})
    greet({"shot": partner})

    @pl.when(at_end)
    def _():
        greet({"shot": partner, "dom": inside})

    @pl.when(passes)
    def _():
        greet({"shot": partner, "dom": outside})

    @pl.when(has_low)
    def _():
        greet({"dom": dom - 1})

    @pl.when(has_high)
    def _():
        greet({"dom": dom + 1})

    loads = [
        pltpu.make_async_copy(labels_hbm, labels, load_sem.at[0]),
        pltpu.make_async_copy(near_hbm.at[0], aa.at[1], load_sem.at[1]),
        pltpu.make_async_copy(current_hbm.at[0], ue.at[0, pl.ds(4, planes)], load_sem.at[2]),
        pltpu.make_async_copy(before_hbm.at[0], u0, load_sem.at[3]),
        pltpu.make_async_copy(far_hbm.at[0], aa.at[0], load_sem.at[4]),
        pltpu.make_async_copy(table_hbm, table, load_sem.at[5]),
        pltpu.make_async_copy(source_hbm, source, load_sem.at[6]),
        pltpu.make_async_copy(wavelet_hbm, wavelet, load_sem.at[7]),
        pltpu.make_async_copy(receivers_hbm, receivers, load_sem.at[8]),
        pltpu.make_async_copy(residual_hbm, residual, load_sem.at[9]),
    ]
    for k in (5, 0, 1, 2, 3, 6, 7, 8, 9, 4):
        loads[k].start()

    peers = 2 + jnp.where(at_end | passes, 1, 0) + jnp.where(has_low, 1, 0) + jnp.where(has_high, 1, 0)
    pl.semaphore_wait(barrier, peers)

    def to_low(e, source_ref):
        buffer = ue.at[e] if e < 4 else se.at[e - 4]
        return pltpu.make_async_remote_copy(
            source_ref, buffer.at[pl.ds(planes + 4, 4)], send_sem.at[0, e], recv_sem.at[0, e],
            device_id={"dom": dom - 1}, device_id_type=MESH,
        )

    def to_high(e, source_ref):
        buffer = ue.at[e] if e < 4 else se.at[e - 4]
        return pltpu.make_async_remote_copy(
            source_ref, buffer.at[pl.ds(0, 4)], send_sem.at[1, e], recv_sem.at[1, e],
            device_id={"dom": dom + 1}, device_id_type=MESH,
        )

    def low_edge(e):
        if e == 0:
            return current_hbm.at[0, pl.ds(0, 4)]
        return (ue.at[e] if e < 4 else se.at[e - 4]).at[pl.ds(4, 4)]

    def high_edge(e):
        if e == 0:
            return current_hbm.at[0, pl.ds(planes - 4, 4)]
        return (ue.at[e] if e < 4 else se.at[e - 4]).at[pl.ds(planes, 4)]

    def send_low(e):
        @pl.when(has_low)
        def _():
            to_low(e, low_edge(e)).start()

    def send_high(e):
        @pl.when(has_high)
        def _():
            to_high(e, high_edge(e)).start()

    def wait_low(e):
        @pl.when(has_low)
        def _():
            to_high(e, high_edge(e)).wait_recv()

    def wait_high(e):
        @pl.when(has_high)
        def _():
            to_low(e, low_edge(e)).wait_recv()

    send_low(0)
    send_high(0)

    @pl.when(dom == 0)
    def _():
        for e in range(4):
            ue[e, 0:4] = jnp.zeros((4, depth, across), F32)
            se[e, 0:4] = jnp.zeros((4, depth, across), F32)

    @pl.when(dom == doms - 1)
    def _():
        for e in range(4):
            ue[e, planes + 4:planes + 8] = jnp.zeros((4, depth, across), F32)
            se[e, planes + 4:planes + 8] = jnp.zeros((4, depth, across), F32)

    loads[5].wait()
    speeds = [table[k] * (1.0 / scale) for k in range(table.shape[0])]
    loads[0].wait()
    loads[1].wait()

    def first_plane(p):
        def rows(i, _):
            r = pl.ds(pl.multiple_of(i * 16, 16), 16)
            region = labels[p, r, :]
            speed = jnp.full(region.shape, speeds[0], F32)
            for k in range(1, len(speeds)):
                speed = jnp.where(region == k, speeds[k], speed)
            rate[p, r, :] = speed
            se[0, p + 4, r, :] = speed * aa[1, p, r, :]
            return 0

        lax.fori_loop(0, depth // 16, rows, 0)

    def first_group(base):
        lax.fori_loop(0, 4, lambda j, c: (first_plane(base + j), c)[1], 0)

    first_group(0)
    send_low(4)
    first_group(planes - 4)
    send_high(4)
    lax.fori_loop(4, planes - 4, lambda p, c: (first_plane(p), c)[1], 0)

    along_y[...] = band(across, across, 0)
    plane_band = band(4 * depth, 4 * depth, depth)
    for k in range(3):
        along_z[:, k * 4 * depth:(k + 1) * 4 * depth] = plane_band

    for k in range(6, 10):
        loads[k].wait()
    row = lax.broadcasted_iota(jnp.int32, (depth, across), 0)
    column = lax.broadcasted_iota(jnp.int32, (depth, across), 1)
    spot[...] = jnp.where((row == source[0, 1]) & (column == source[0, 2]), 1.0, 0.0).astype(F32)
    source_plane = source[0, 0] - dom * planes

    def across_stage(ext, out):
        def group(g, _):
            for q in range(4):
                def rows(i, _, q=q):
                    at = pl.multiple_of(i * 16, 16)
                    parts = split(ext[4 + 4 * g + q, pl.ds(at, 16), :])
                    for k in range(3):
                        stack[pl.ds(pl.multiple_of(at + (4 * k + q) * depth, 16), 16), :] = parts[k]
                    return 0

                lax.fori_loop(0, depth // 16, rows, 0, unroll=True)
            size = 4 * depth
            in_y = jnp.dot(stack[...], along_y[...], preferred_element_type=F32)
            in_z = jnp.dot(along_z[...], stack[...], preferred_element_type=F32)
            both = (in_y[2 * size:] + in_y[size:2 * size]) + in_y[:size] + in_z
            out[pl.ds(4 * g, 4)] = both.reshape(4, depth, across)
            return 0

        lax.fori_loop(0, groups, group, 0)

    def laplace(planes_of, j, rest):
        result = rest + centre * planes_of[j + 4]
        for k in range(1, 5):
            result = result + sides[k - 1] * (planes_of[j + 4 + k] + planes_of[j + 4 - k])
        return result

    def forward_group(n, g):
        pulses = [jnp.where(source_plane == 4 * g + j, wavelet[0, n], 0.0) for j in range(4)]

        def rows(i, _):
            r = pl.ds(pl.multiple_of(i * 8, 8), 8)
            window = [ue[n, 4 * g + q, r, :] for q in range(12)]
            for j in range(4):
                p = 4 * g + j
                curve = laplace(window, j, yzf[p, r, :])
                if n == 3:
                    grad[p, r, :] = grad[p, r, :] + aa[1, p, r, :] * curve
                else:
                    lap[n, p, r, :] = curve
                previous = u0[p, r, :] if n == 0 else ue[n - 1, p + 4, r, :]
                upcoming = 2.0 * window[j + 4] - previous + rate[p, r, :] * curve
                upcoming = upcoming + pulses[j] * spot[r, :]
                if n == 3:
                    final[0, p, r, :] = upcoming
                else:
                    ue[n + 1, p + 4, r, :] = upcoming
            return 0

        lax.fori_loop(0, depth // 8, rows, 0)

    def adjoint_group(m, g):
        def rows(i, _):
            r = pl.ds(pl.multiple_of(i * 8, 8), 8)
            window = [se[m, 4 * g + q, r, :] for q in range(12)]
            for j in range(4):
                p = 4 * g + j
                curve = laplace(window, j, yza[p, r, :])
                earlier = 2.0 * aa[m + 1, p, r, :] - aa[m, p, r, :] + curve + inject[3 - m, p, r, :]
                if m == 3:
                    first[0, p, r, :] = earlier
                else:
                    aa[m + 2, p, r, :] = earlier
                    se[m + 1, p + 4, r, :] = rate[p, r, :] * earlier
            return 0

        lax.fori_loop(0, depth // 8, rows, 0)

    def middle(one, n):
        lax.fori_loop(1, groups - 1, lambda g, c: (one(n, g), c)[1], 0)

    cell = (receivers[0] - dom * planes) * depth + receivers[1]

    def onehot_rows(i, _):
        at = pl.multiple_of(i * 16, 16)
        here = lax.broadcasted_iota(jnp.int32, (16, recs), 0) + at
        onehot[pl.ds(at, 16), :] = jnp.where(here == cell, 1.0, 0.0).astype(BF16)
        return 0

    lax.fori_loop(0, planes * depth // 16, onehot_rows, 0)

    def inject_step(n, _):
        value = residual[pl.ds(n, 1), :]
        parts = [part.astype(F32) for part in split(value)]

        def columns(i, _):
            at = pl.multiple_of(i * 16, 16)
            here = lax.broadcasted_iota(jnp.int32, (16, recs), 0) + at == receivers[2]
            for k in range(3):
                amounts[pl.ds(pl.multiple_of(at + k * across, 16), 16), :] = jnp.where(here, parts[k], 0.0).astype(BF16)
            return 0

        lax.fori_loop(0, across // 16, columns, 0)

        def group(g, _):
            rows = pl.ds(pl.multiple_of(g * 4 * depth, 4 * depth), 4 * depth)
            spread = lax.dot_general(
                onehot[rows, :], amounts[...], (((1,), (1,)), ((), ())), preferred_element_type=F32
            )
            both = (spread[:, 2 * across:] + spread[:, across:2 * across]) + spread[:, :across]
            inject[n, pl.ds(4 * g, 4)] = both.reshape(4, depth, across)
            return 0

        lax.fori_loop(0, groups, group, 0)
        return 0

    def combine(p, _):
        def rows(i, _):
            r = pl.ds(pl.multiple_of(i * 16, 16), 16)
            value = aa[2, p, r, :] * lap[2, p, r, :]
            for n in (1, 0):
                value = value + aa[4 - n, p, r, :] * lap[n, p, r, :]
            grad[p, r, :] = value
            return 0

        lax.fori_loop(0, depth // 16, rows, 0)
        return 0

    mine, other = 4 + 4 * core, 8 - 4 * core
    mine_edge, other_edge = (planes - 4) * core, (planes - 4) * (1 - core)

    def gradient_copy(phase, chunk, source_ref, target_ref, device):
        return pltpu.make_async_remote_copy(
            source_ref, target_ref, gsend_sem.at[phase, chunk], grecv_sem.at[phase, chunk],
            device_id=device, device_id_type=MESH,
        )

    def to_sibling():
        return gradient_copy(0, 0, grad.at[pl.ds(other, 4)], near_grad.at[pl.ds(0, 4)], {"shot": sibling})

    def to_partner():
        return gradient_copy(1, 0, partial.at[pl.ds(0, 4)], far_grad.at[pl.ds(0, 4)], {"shot": partner})

    def to_passer():
        return gradient_copy(3, 0, partial.at[pl.ds(0, 4)], passing, {"shot": partner, "dom": inside})

    def pass_on():
        return gradient_copy(4, 0, passing, far_grad.at[pl.ds(0, 4)], {"dom": outside})

    def total_to_sibling():
        place_of = gradient.at[pl.ds(mine, 4)]
        return gradient_copy(2, 0, place_of, place_of, {"shot": sibling})

    def edge_to_sibling(j):
        return gradient_copy(0, 1 + j, grad.at[other_edge + j], near_grad.at[4 + j], {"shot": sibling})

    def edge_to_partner(j):
        return gradient_copy(1, 1 + j, partial.at[4 + j], far_grad.at[4 + j], {"shot": partner})

    def edge_total_to_sibling(j):
        place_of = gradient.at[mine_edge + j]
        return gradient_copy(2, 1 + j, place_of, place_of, {"shot": sibling})

    def sum_near():
        to_sibling().wait_recv()

        def one(j, _):
            partial[j] = grad[mine + j] + near_grad[j]
            return 0

        lax.fori_loop(0, 4, one, 0)

        @pl.when(at_end)
        def _():
            to_passer().start()

        @pl.when(jnp.logical_not(at_end))
        def _():
            to_partner().start()

    def sum_far():
        @pl.when(at_end)
        def _():
            pass_on().wait_recv()

        @pl.when(jnp.logical_not(at_end))
        def _():
            to_partner().wait_recv()

        def one(j, _):
            gradient[mine + j] = (partial[j] + far_grad[j]) * (1.0 / scale)
            return 0

        lax.fori_loop(0, 4, one, 0)
        total_to_sibling().start()

    def sum_near_edge():
        for j in range(4):
            edge_to_sibling(j).wait_recv()
            partial[4 + j] = grad[mine_edge + j] + near_grad[4 + j]
            edge_to_partner(j).start()

    def sum_far_edge():
        for j in range(4):
            edge_to_partner(j).wait_recv()
            gradient[mine_edge + j] = (partial[4 + j] + far_grad[4 + j]) * (1.0 / scale)
            edge_total_to_sibling(j).start()

    loads[2].wait()
    across_stage(ue.at[0], yzf)
    loads[3].wait()
    middle(forward_group, 0)

    for n in range(4):
        wait_low(n)
        forward_group(n, 0)
        if n < 3:
            send_low(n + 1)
        wait_high(n)
        forward_group(n, groups - 1)
        if n < 3:
            send_high(n + 1)
            across_stage(ue.at[n + 1], yzf)
            if n == 2:
                lax.fori_loop(4, planes - 4, combine, 0)
            middle(forward_group, n + 1)
        if n == 0:
            loads[4].wait()
            lax.fori_loop(3, 4, inject_step, 0)
            across_stage(se.at[0], yza)
            middle(adjoint_group, 0)
        if n == 2:
            to_sibling().start()
            sum_near()
        if n == 3:
            for j in range(4):
                edge_to_sibling(j).start()

            @pl.when(passes)
            def _():
                to_passer().wait_recv()
                pass_on().start()

            sum_near_edge()
        if n == 1:
            lax.fori_loop(1, 2, inject_step, 0)
        wait_low(n + 4)
        adjoint_group(n, 0)
        if n < 3:
            send_low(n + 5)
        wait_high(n + 4)
        adjoint_group(n, groups - 1)
        if n < 3:
            send_high(n + 5)
        if n < 2:
            lax.fori_loop(2 - 2 * n, 3 - 2 * n, inject_step, 0)
        if n < 3:
            across_stage(se.at[n + 1], yza)
            middle(adjoint_group, n + 1)
        if n == 2:
            lax.fori_loop(0, 4, combine, 0)
            lax.fori_loop(planes - 4, planes, combine, 0)
    sum_far()
    sum_far_edge()

    total_to_sibling().wait_recv()
    for j in range(4):
        edge_total_to_sibling(j).wait_recv()
    for e in range(8):
        @pl.when(has_low)
        def _():
            to_low(e, low_edge(e)).wait_send()

        @pl.when(has_high)
        def _():
            to_high(e, high_edge(e)).wait_send()
    to_sibling().wait_send()
    total_to_sibling().wait_send()

    @pl.when(at_end)
    def _():
        to_passer().wait_send()

    @pl.when(passes)
    def _():
        pass_on().wait_send()

    @pl.when(jnp.logical_not(at_end))
    def _():
        to_partner().wait_send()

    for j in range(4):
        edge_to_sibling(j).wait_send()
        edge_to_partner(j).wait_send()
        edge_total_to_sibling(j).wait_send()


def write(*refs):
    sems = refs[6]
    copies = []
    for k in range(3):
        source_ref, target_ref = refs[k], refs[k + 3]
        if k < 2:
            source_ref, target_ref = source_ref.at[0], target_ref.at[0]
        size = source_ref.shape[0] // 4
        for part in range(4):
            piece = pl.ds(part * size, size)
            copies.append(pltpu.make_async_copy(source_ref.at[piece], target_ref.at[piece], sems.at[k, part]))
    for copy in copies:
        copy.start()
    for copy in copies:
        copy.wait()


def per_device(
    doms, wave_before, wave_current, adjoint_far, adjoint_near, labels, table,
    source_index, wavelet, receiver_index, residual,
):
    block = wave_current.shape
    planes, depth, across = labels.shape
    recs = receiver_index.shape[1]
    field = (planes, depth, across)
    extended = (4, planes + 8, depth, across)
    whole = pl.BlockSpec(memory_space=pltpu.HBM)
    vectors = pl.BlockSpec(memory_space=pltpu.VMEM)
    results = pl.pallas_call(
        functools.partial(kernel, doms),
        out_shape=(
            pltpu.VMEM(block, F32),
            pltpu.VMEM(block, F32),
            pltpu.VMEM(field, F32),
        ),
        in_specs=[whole] * 10,
        out_specs=(vectors, vectors, vectors),
        scratch_shapes=[
            pltpu.SMEM(table.shape, F32),
            pltpu.SMEM(source_index.shape, jnp.int32),
            pltpu.SMEM(wavelet.shape, F32),
            pltpu.VMEM((3, 1, recs), jnp.int32),
            pltpu.VMEM(residual.shape[1:], F32),
            pltpu.VMEM(extended, F32),
            pltpu.VMEM(field, F32),
            pltpu.VMEM(extended, F32),
            pltpu.VMEM((5,) + field, F32),
            pltpu.VMEM((3,) + field, F32),
            pltpu.VMEM(field, F32),
            pltpu.VMEM(field, jnp.int32),
            pltpu.VMEM(field, F32),
            pltpu.VMEM(field, F32),
            pltpu.VMEM((12 * depth, across), BF16),
            pltpu.VMEM((across, across), BF16),
            pltpu.VMEM((4 * depth, 12 * depth), BF16),
            pltpu.VMEM((planes * depth, recs), BF16),
            pltpu.VMEM((3 * across, recs), BF16),
            pltpu.VMEM((4,) + field, F32),
            pltpu.VMEM((depth, across), F32),
            pltpu.VMEM(field, F32),
            pltpu.VMEM((8, depth, across), F32),
            pltpu.VMEM((8, depth, across), F32),
            pltpu.VMEM((8, depth, across), F32),
            pltpu.VMEM((4, depth, across), F32),
            pltpu.SemaphoreType.DMA((10,)),
            pltpu.SemaphoreType.DMA((2, 8)),
            pltpu.SemaphoreType.DMA((2, 8)),
            pltpu.SemaphoreType.DMA((5, 5)),
            pltpu.SemaphoreType.DMA((5, 5)),
        ],
        compiler_params=pltpu.CompilerParams(
            collective_id=0, has_side_effects=True, vmem_limit_bytes=60 << 20
        ),
        name="window",
    )(
        wave_before, wave_current, adjoint_far, adjoint_near, labels, table,
        source_index, wavelet, jnp.transpose(receiver_index, (2, 0, 1)), residual[0],
    )
    held = [pltpu.with_memory_space_constraint(result, pltpu.VMEM) for result in results]
    return pl.pallas_call(
        write,
        out_shape=tuple(jax.ShapeDtypeStruct(result.shape, F32) for result in results),
        in_specs=[vectors] * 3,
        out_specs=(whole,) * 3,
        scratch_shapes=[pltpu.SemaphoreType.DMA((3, 4))],
        compiler_params=pltpu.CompilerParams(vmem_limit_bytes=1 << 20),
        name="write",
    )(*held)


def solution(mesh):
    fields = P("shot", "dom", None, None)
    return jax.shard_map(
        functools.partial(per_device, mesh.shape["dom"]),
        mesh=mesh,
        in_specs=(
            fields, fields, fields, fields, P("dom", None, None), P(),
            P("shot", None), P("shot", None), P("shot", None, None), P("shot", None, None),
        ),
        out_specs=(fields, fields, P("dom", None, None)),
        check_vma=False,
    )
```

```python
import functools

import jax
import jax.numpy as jnp
import numpy as np
from jax import lax
from jax.experimental import pallas as pl
from jax.experimental.pallas import tpu as pltpu
from jax.sharding import PartitionSpec as P

MESH = pl.DeviceIdType.MESH
F32 = jnp.float32
BF16 = jnp.bfloat16

ring = 8

scale = 5040.0
centre = 3.0 * -14350.0
sides = (8064.0, -1008.0, 128.0, -9.0)


def split(values):
    high = values.astype(BF16)
    rest = values - high.astype(F32)
    middle = rest.astype(BF16)
    low = (rest - middle.astype(F32)).astype(BF16)
    return high, middle, low


def band(size):
    row = lax.broadcasted_iota(jnp.int32, (size, size), 0)
    column = lax.broadcasted_iota(jnp.int32, (size, size), 1)
    away = jnp.abs(row - column)
    result = jnp.zeros((size, size), F32)
    for k in range(1, 5):
        result = jnp.where(away == k, sides[k - 1], result)
    return result.astype(BF16)


def kernel(
    doms,
    before_hbm, current_hbm, far_hbm, near_hbm, labels_hbm,
    table_hbm, source_hbm, wavelet_hbm, receivers_hbm, residual_hbm,
    final, first, gradient,
    table, source, wavelet, receivers, residual, ue, u0, se, aa, lap, rate, labels, yzf, yza, wide, tall, along_y, along_z,
    onehot, amounts, inject, spot, grad, near_grad, far_grad, partial, passing,
    load_sem, send_sem, recv_sem, gsend_sem, grecv_sem,
):
    shot = lax.axis_index("shot")
    dom = lax.axis_index("dom")
    planes, depth, across = u0.shape
    groups = planes // 4
    recs = receivers.shape[2]
    core = lax.rem(shot, 2)
    sibling = shot + 1 - 2 * core
    partner = lax.rem(shot + 2, 4)
    place = lax.rem(dom, ring)
    at_end = (place == 0) | (place == ring - 1)
    passes = (place == 1) | (place == ring - 2)
    inside = jnp.where(place == 0, dom + 1, dom - 1)
    outside = jnp.where(place == 1, dom - 1, dom + 1)
    has_low = dom > 0
    has_high = dom < doms - 1

    barrier = pltpu.get_barrier_semaphore()

    def greet(device):
        pl.semaphore_signal(barrier, inc=1, device_id=device, device_id_type=MESH)

    greet({"shot": sibling})
    greet({"shot": partner})

    @pl.when(at_end)
    def _():
        greet({"shot": partner, "dom": inside})

    @pl.when(passes)
    def _():
        greet({"shot": partner, "dom": outside})

    @pl.when(has_low)
    def _():
        greet({"dom": dom - 1})

    @pl.when(has_high)
    def _():
        greet({"dom": dom + 1})

    loads = [
        pltpu.make_async_copy(labels_hbm, labels, load_sem.at[0]),
        pltpu.make_async_copy(near_hbm.at[0], aa.at[1], load_sem.at[1]),
        pltpu.make_async_copy(current_hbm.at[0], ue.at[0, pl.ds(4, planes)], load_sem.at[2]),
        pltpu.make_async_copy(before_hbm.at[0], u0, load_sem.at[3]),
        pltpu.make_async_copy(far_hbm.at[0], aa.at[0], load_sem.at[4]),
        pltpu.make_async_copy(table_hbm, table, load_sem.at[5]),
        pltpu.make_async_copy(source_hbm, source, load_sem.at[6]),
        pltpu.make_async_copy(wavelet_hbm, wavelet, load_sem.at[7]),
        pltpu.make_async_copy(receivers_hbm, receivers, load_sem.at[8]),
        pltpu.make_async_copy(residual_hbm, residual, load_sem.at[9]),
    ]
    for k in (5, 0, 1, 2, 3, 6, 7, 8, 9, 4):
        loads[k].start()

    peers = 2 + jnp.where(at_end | passes, 1, 0) + jnp.where(has_low, 1, 0) + jnp.where(has_high, 1, 0)
    pl.semaphore_wait(barrier, peers)

    def to_low(e, source_ref):
        buffer = ue.at[e] if e < 4 else se.at[e - 4]
        return pltpu.make_async_remote_copy(
            source_ref, buffer.at[pl.ds(planes + 4, 4)], send_sem.at[0, e], recv_sem.at[0, e],
            device_id={"dom": dom - 1}, device_id_type=MESH,
        )

    def to_high(e, source_ref):
        buffer = ue.at[e] if e < 4 else se.at[e - 4]
        return pltpu.make_async_remote_copy(
            source_ref, buffer.at[pl.ds(0, 4)], send_sem.at[1, e], recv_sem.at[1, e],
            device_id={"dom": dom + 1}, device_id_type=MESH,
        )

    def low_edge(e):
        if e == 0:
            return current_hbm.at[0, pl.ds(0, 4)]
        return (ue.at[e] if e < 4 else se.at[e - 4]).at[pl.ds(4, 4)]

    def high_edge(e):
        if e == 0:
            return current_hbm.at[0, pl.ds(planes - 4, 4)]
        return (ue.at[e] if e < 4 else se.at[e - 4]).at[pl.ds(planes, 4)]

    def send(e, high):
        @pl.when(jnp.logical_not(high) & has_low)
        def _():
            to_low(e, low_edge(e)).start()

        @pl.when(high & has_high)
        def _():
            to_high(e, high_edge(e)).start()

    def wait(e, high):
        @pl.when(jnp.logical_not(high) & has_low)
        def _():
            to_high(e, high_edge(e)).wait_recv()

        @pl.when(high & has_high)
        def _():
            to_low(e, low_edge(e)).wait_recv()

    order = (place == 0, place != 0)

    def edge_group(high):
        return jnp.where(high, groups - 1, 0)

    for high in order:
        send(0, high)

    @pl.when(dom == 0)
    def _():
        for e in range(4):
            ue[e, 0:4] = jnp.zeros((4, depth, across), F32)
            se[e, 0:4] = jnp.zeros((4, depth, across), F32)

    @pl.when(dom == doms - 1)
    def _():
        for e in range(4):
            ue[e, planes + 4:planes + 8] = jnp.zeros((4, depth, across), F32)
            se[e, planes + 4:planes + 8] = jnp.zeros((4, depth, across), F32)

    loads[5].wait()
    speeds = [table[k] * (1.0 / scale) for k in range(table.shape[0])]
    loads[0].wait()
    loads[1].wait()

    def first_plane(p):
        def rows(i, _):
            r = pl.ds(pl.multiple_of(i * 16, 16), 16)
            region = labels[p, r, :]
            speed = jnp.full(region.shape, speeds[0], F32)
            for k in range(1, len(speeds)):
                speed = jnp.where(region == k, speeds[k], speed)
            rate[p, r, :] = speed
            se[0, p + 4, r, :] = speed * aa[1, p, r, :]
            return 0

        lax.fori_loop(0, depth // 16, rows, 0)

    def first_group(base):
        lax.fori_loop(0, 4, lambda j, c: (first_plane(base + j), c)[1], 0)

    for high in order:
        first_group(4 * edge_group(high))
        send(4, high)
    lax.fori_loop(4, planes - 4, lambda p, c: (first_plane(p), c)[1], 0)

    row_band, column_band = band(across), band(depth)
    for k in range(3):
        along_y[k * across:(k + 1) * across, :] = row_band
        along_z[:, k * depth:(k + 1) * depth] = column_band

    for k in range(6, 10):
        loads[k].wait()
    row = lax.broadcasted_iota(jnp.int32, (depth, across), 0)
    column = lax.broadcasted_iota(jnp.int32, (depth, across), 1)
    spot[...] = jnp.where((row == source[0, 1]) & (column == source[0, 2]), 1.0, 0.0).astype(F32)
    source_plane = source[0, 0] - dom * planes

    def across_stage(ext, out):
        def pair(i, _):
            for h in range(2):
                g = 2 * i + h
                for q in range(4):
                    for part in range(depth // 16):
                        at = 16 * part
                        terms = split(ext[4 + 4 * g + q, at:at + 16, :])
                        for k in range(3):
                            wide[h, q * depth + at:q * depth + at + 16, k * across:(k + 1) * across] = terms[k]
                            tall[h, q, k * depth + at:k * depth + at + 16, :] = terms[k]
                in_y = jnp.dot(wide[h], along_y[...], preferred_element_type=F32)
                for q in range(4):
                    in_z = jnp.dot(along_z[...], tall[h, q], preferred_element_type=F32)
                    out[4 * g + q] = in_y[q * depth:(q + 1) * depth] + in_z
            return 0

        lax.fori_loop(0, groups // 2, pair, 0)

    def laplace(planes_of, j, rest):
        result = rest + centre * planes_of[j + 4]
        for k in range(1, 5):
            result = result + sides[k - 1] * (planes_of[j + 4 + k] + planes_of[j + 4 - k])
        return result

    def forward_group(n, g):
        pulses = [jnp.where(source_plane == 4 * g + j, wavelet[0, n], 0.0) for j in range(4)]

        def rows(i, _):
            r = pl.ds(pl.multiple_of(i * 8, 8), 8)
            window = [ue[n, 4 * g + q, r, :] for q in range(12)]
            for j in range(4):
                p = 4 * g + j
                curve = laplace(window, j, yzf[p, r, :])
                if n == 3:
                    grad[p, r, :] = grad[p, r, :] + aa[1, p, r, :] * curve
                else:
                    lap[n, p, r, :] = curve
                previous = u0[p, r, :] if n == 0 else ue[n - 1, p + 4, r, :]
                upcoming = 2.0 * window[j + 4] - previous + rate[p, r, :] * curve
                upcoming = upcoming + pulses[j] * spot[r, :]
                if n == 3:
                    final[0, p, r, :] = upcoming
                else:
                    ue[n + 1, p + 4, r, :] = upcoming
            return 0

        lax.fori_loop(0, depth // 8, rows, 0)

    def adjoint_group(m, g):
        def rows(i, _):
            r = pl.ds(pl.multiple_of(i * 8, 8), 8)
            window = [se[m, 4 * g + q, r, :] for q in range(12)]
            for j in range(4):
                p = 4 * g + j
                curve = laplace(window, j, yza[p, r, :])
                earlier = 2.0 * aa[m + 1, p, r, :] - aa[m, p, r, :] + curve + inject[3 - m, p, r, :]
                if m == 3:
                    first[0, p, r, :] = earlier
                else:
                    aa[m + 2, p, r, :] = earlier
                    se[m + 1, p + 4, r, :] = rate[p, r, :] * earlier
            return 0

        lax.fori_loop(0, depth // 8, rows, 0)

    def middle(one, n):
        lax.fori_loop(1, groups - 1, lambda g, c: (one(n, g), c)[1], 0)

    cell = (receivers[0] - dom * planes) * depth + receivers[1]

    def onehot_rows(i, _):
        at = pl.multiple_of(i * 16, 16)
        here = lax.broadcasted_iota(jnp.int32, (16, recs), 0) + at
        onehot[pl.ds(at, 16), :] = jnp.where(here == cell, 1.0, 0.0).astype(BF16)
        return 0

    lax.fori_loop(0, planes * depth // 16, onehot_rows, 0)

    def inject_step(n):
        value = residual[n:n + 1, :]
        high = value.astype(BF16).astype(F32)
        parts = (high, (value - high).astype(BF16).astype(F32))

        def columns(i, _):
            at = pl.multiple_of(i * 16, 16)
            here = lax.broadcasted_iota(jnp.int32, (16, recs), 0) + at == receivers[2]
            for k in range(2):
                amounts[pl.ds(pl.multiple_of(at + k * across, 16), 16), :] = jnp.where(here, parts[k], 0.0).astype(BF16)
            return 0

        lax.fori_loop(0, across // 16, columns, 0)

        def half(i, _):
            rows = pl.ds(pl.multiple_of(i * 8 * depth, 8 * depth), 8 * depth)
            spread = lax.dot_general(
                onehot[rows, :], amounts[...], (((1,), (1,)), ((), ())), preferred_element_type=F32
            )
            both = spread[:, across:] + spread[:, :across]
            inject[n, pl.ds(8 * i, 8)] = both.reshape(8, depth, across)
            return 0

        lax.fori_loop(0, planes // 8, half, 0)

    def combine(p, _):
        def rows(i, _):
            r = pl.ds(pl.multiple_of(i * 16, 16), 16)
            value = aa[2, p, r, :] * lap[2, p, r, :]
            for n in (1, 0):
                value = value + aa[4 - n, p, r, :] * lap[n, p, r, :]
            grad[p, r, :] = value
            return 0

        lax.fori_loop(0, depth // 16, rows, 0)
        return 0

    mine, other = 4 + 4 * core, 8 - 4 * core
    mine_edge, other_edge = (planes - 4) * core, (planes - 4) * (1 - core)

    def gradient_copy(phase, chunk, source_ref, target_ref, device):
        return pltpu.make_async_remote_copy(
            source_ref, target_ref, gsend_sem.at[phase, chunk], grecv_sem.at[phase, chunk],
            device_id=device, device_id_type=MESH,
        )

    def to_sibling():
        return gradient_copy(0, 0, grad.at[pl.ds(other, 4)], near_grad.at[pl.ds(0, 4)], {"shot": sibling})

    def to_partner():
        return gradient_copy(1, 0, partial.at[pl.ds(0, 4)], far_grad.at[pl.ds(0, 4)], {"shot": partner})

    def to_passer():
        return gradient_copy(3, 0, partial.at[pl.ds(0, 4)], passing, {"shot": partner, "dom": inside})

    def pass_on():
        return gradient_copy(4, 0, passing, far_grad.at[pl.ds(0, 4)], {"dom": outside})

    def total_to_sibling():
        place_of = gradient.at[pl.ds(mine, 4)]
        return gradient_copy(2, 0, place_of, place_of, {"shot": sibling})

    def edge_to_sibling(j):
        return gradient_copy(0, 1 + j, grad.at[other_edge + j], near_grad.at[4 + j], {"shot": sibling})

    def edge_to_partner(j):
        return gradient_copy(1, 1 + j, partial.at[4 + j], far_grad.at[4 + j], {"shot": partner})

    def edge_total_to_sibling(j):
        place_of = gradient.at[mine_edge + j]
        return gradient_copy(2, 1 + j, place_of, place_of, {"shot": sibling})

    def sum_near():
        to_sibling().wait_recv()

        def one(j, _):
            partial[j] = grad[mine + j] + near_grad[j]
            return 0

        lax.fori_loop(0, 4, one, 0)

        @pl.when(at_end)
        def _():
            to_passer().start()

        @pl.when(jnp.logical_not(at_end))
        def _():
            to_partner().start()

    def sum_far():
        @pl.when(at_end)
        def _():
            pass_on().wait_recv()

        @pl.when(jnp.logical_not(at_end))
        def _():
            to_partner().wait_recv()

        def one(j, _):
            gradient[mine + j] = (partial[j] + far_grad[j]) * (1.0 / scale)
            return 0

        lax.fori_loop(0, 4, one, 0)
        total_to_sibling().start()

    def sum_near_edge(high):
        owner = high == (core == 1)

        @pl.when(jnp.logical_not(owner))
        def _():
            for j in range(4):
                edge_to_sibling(j).start()

        @pl.when(owner)
        def _():
            for j in range(4):
                edge_to_sibling(j).wait_recv()
                partial[4 + j] = grad[mine_edge + j] + near_grad[4 + j]
                edge_to_partner(j).start()

    def sum_far_edge():
        for j in range(4):
            edge_to_partner(j).wait_recv()
            gradient[mine_edge + j] = (partial[4 + j] + far_grad[4 + j]) * (1.0 / scale)
            edge_total_to_sibling(j).start()

    loads[2].wait()
    across_stage(ue.at[0], yzf)
    loads[3].wait()
    middle(forward_group, 0)
    inject_step(3)
    loads[4].wait()
    across_stage(se.at[0], yza)
    middle(adjoint_group, 0)

    for n in range(4):
        for high in order:
            wait(n, high)
            forward_group(n, edge_group(high))
            if n < 3:
                send(n + 1, high)
            else:
                sum_near_edge(high)
        if n < 3:
            across_stage(ue.at[n + 1], yzf)
            if n == 2:
                lax.fori_loop(4, planes - 4, combine, 0)
            middle(forward_group, n + 1)
        if n == 2:
            to_sibling().start()
            sum_near()
        if n == 3:
            @pl.when(passes)
            def _():
                to_passer().wait_recv()
                pass_on().start()
        if n < 2:
            inject_step(2 - n)
        for high in order:
            wait(n + 4, high)
            adjoint_group(n, edge_group(high))
            if n < 3:
                send(n + 5, high)
        if n == 1:
            inject_step(0)
        if n < 3:
            across_stage(se.at[n + 1], yza)
            middle(adjoint_group, n + 1)
        if n == 2:
            lax.fori_loop(0, 4, combine, 0)
            lax.fori_loop(planes - 4, planes, combine, 0)
    sum_far_edge()
    sum_far()

    total_to_sibling().wait_recv()
    for j in range(4):
        edge_total_to_sibling(j).wait_recv()
    for e in range(8):
        @pl.when(has_low)
        def _():
            to_low(e, low_edge(e)).wait_send()

        @pl.when(has_high)
        def _():
            to_high(e, high_edge(e)).wait_send()
    to_sibling().wait_send()
    total_to_sibling().wait_send()

    @pl.when(at_end)
    def _():
        to_passer().wait_send()

    @pl.when(passes)
    def _():
        pass_on().wait_send()

    @pl.when(jnp.logical_not(at_end))
    def _():
        to_partner().wait_send()

    for j in range(4):
        edge_to_sibling(j).wait_send()
        edge_to_partner(j).wait_send()
        edge_total_to_sibling(j).wait_send()


def write(*refs):
    sems = refs[6]
    copies = []
    for k in range(3):
        source_ref, target_ref = refs[k], refs[k + 3]
        if k < 2:
            source_ref, target_ref = source_ref.at[0], target_ref.at[0]
        size = source_ref.shape[0] // 4
        for part in range(4):
            piece = pl.ds(part * size, size)
            copies.append(pltpu.make_async_copy(source_ref.at[piece], target_ref.at[piece], sems.at[k, part]))
    for copy in copies:
        copy.start()
    for copy in copies:
        copy.wait()


def per_device(
    doms, wave_before, wave_current, adjoint_far, adjoint_near, labels, table,
    source_index, wavelet, receiver_index, residual,
):
    block = wave_current.shape
    planes, depth, across = labels.shape
    recs = receiver_index.shape[1]
    field = (planes, depth, across)
    extended = (4, planes + 8, depth, across)
    whole = pl.BlockSpec(memory_space=pltpu.HBM)
    vectors = pl.BlockSpec(memory_space=pltpu.VMEM)
    results = pl.pallas_call(
        functools.partial(kernel, doms),
        out_shape=(
            pltpu.VMEM(block, F32),
            pltpu.VMEM(block, F32),
            pltpu.VMEM(field, F32),
        ),
        in_specs=[whole] * 10,
        out_specs=(vectors, vectors, vectors),
        scratch_shapes=[
            pltpu.SMEM(table.shape, F32),
            pltpu.SMEM(source_index.shape, jnp.int32),
            pltpu.SMEM(wavelet.shape, F32),
            pltpu.VMEM((3, 1, recs), jnp.int32),
            pltpu.VMEM(residual.shape[1:], F32),
            pltpu.VMEM(extended, F32),
            pltpu.VMEM(field, F32),
            pltpu.VMEM(extended, F32),
            pltpu.VMEM((5,) + field, F32),
            pltpu.VMEM((3,) + field, F32),
            pltpu.VMEM(field, F32),
            pltpu.VMEM(field, jnp.int32),
            pltpu.VMEM(field, F32),
            pltpu.VMEM(field, F32),
            pltpu.VMEM((2, 4 * depth, 3 * across), BF16),
            pltpu.VMEM((2, 4, 3 * depth, across), BF16),
            pltpu.VMEM((3 * across, across), BF16),
            pltpu.VMEM((depth, 3 * depth), BF16),
            pltpu.VMEM((planes * depth, recs), BF16),
            pltpu.VMEM((2 * across, recs), BF16),
            pltpu.VMEM((4,) + field, F32),
            pltpu.VMEM((depth, across), F32),
            pltpu.VMEM(field, F32),
            pltpu.VMEM((8, depth, across), F32),
            pltpu.VMEM((8, depth, across), F32),
            pltpu.VMEM((8, depth, across), F32),
            pltpu.VMEM((4, depth, across), F32),
            pltpu.SemaphoreType.DMA((10,)),
            pltpu.SemaphoreType.DMA((2, 8)),
            pltpu.SemaphoreType.DMA((2, 8)),
            pltpu.SemaphoreType.DMA((5, 5)),
            pltpu.SemaphoreType.DMA((5, 5)),
        ],
        compiler_params=pltpu.CompilerParams(
            collective_id=0, has_side_effects=True, vmem_limit_bytes=60 << 20
        ),
        name="window",
    )(
        wave_before, wave_current, adjoint_far, adjoint_near, labels, table,
        source_index, wavelet, jnp.transpose(receiver_index, (2, 0, 1)), residual[0],
    )
    held = [pltpu.with_memory_space_constraint(result, pltpu.VMEM) for result in results]
    return pl.pallas_call(
        write,
        out_shape=tuple(jax.ShapeDtypeStruct(result.shape, F32) for result in results),
        in_specs=[vectors] * 3,
        out_specs=(whole,) * 3,
        scratch_shapes=[pltpu.SemaphoreType.DMA((3, 4))],
        compiler_params=pltpu.CompilerParams(vmem_limit_bytes=1 << 20),
        name="write",
    )(*held)


def solution(mesh):
    fields = P("shot", "dom", None, None)
    return jax.shard_map(
        functools.partial(per_device, mesh.shape["dom"]),
        mesh=mesh,
        in_specs=(
            fields, fields, fields, fields, P("dom", None, None), P(),
            P("shot", None), P("shot", None), P("shot", None, None), P("shot", None, None),
        ),
        out_specs=(fields, fields, P("dom", None, None)),
        check_vma=False,
    )
```

```python
import functools

import jax
import jax.numpy as jnp
import numpy as np
from jax import lax
from jax.experimental import pallas as pl
from jax.experimental.pallas import tpu as pltpu
from jax.sharding import PartitionSpec as P

MESH = pl.DeviceIdType.MESH
F32 = jnp.float32
BF16 = jnp.bfloat16

ring = 8

scale = 5040.0
centre = 3.0 * -14350.0
sides = (8064.0, -1008.0, 128.0, -9.0)


def split(values):
    high = values.astype(BF16)
    rest = values - high.astype(F32)
    middle = rest.astype(BF16)
    low = (rest - middle.astype(F32)).astype(BF16)
    return high, middle, low


def band(size):
    row = lax.broadcasted_iota(jnp.int32, (size, size), 0)
    column = lax.broadcasted_iota(jnp.int32, (size, size), 1)
    away = jnp.abs(row - column)
    result = jnp.zeros((size, size), F32)
    for k in range(1, 5):
        result = jnp.where(away == k, sides[k - 1], result)
    return result.astype(BF16)


def kernel(
    doms,
    before_hbm, current_hbm, far_hbm, near_hbm, labels_hbm,
    table_hbm, source_hbm, wavelet_hbm, receivers_hbm, residual_hbm,
    final, first, gradient,
    table, source, wavelet, receivers, residual, ue, u0, se, aa, lap, rate, labels, yzf, yza, wide, tall, along_y, along_z,
    onehot, amounts, inject, spot, grad, near_grad, far_grad, partial, passing,
    load_sem, send_sem, recv_sem, gsend_sem, grecv_sem,
):
    shot = lax.axis_index("shot")
    dom = lax.axis_index("dom")
    planes, depth, across = u0.shape
    groups = planes // 4
    recs = receivers.shape[2]
    core = lax.rem(shot, 2)
    sibling = shot + 1 - 2 * core
    partner = lax.rem(shot + 2, 4)
    place = lax.rem(dom, ring)
    at_end = (place == 0) | (place == ring - 1)
    passes = (place == 1) | (place == ring - 2)
    inside = jnp.where(place == 0, dom + 1, dom - 1)
    outside = jnp.where(place == 1, dom - 1, dom + 1)
    has_low = dom > 0
    has_high = dom < doms - 1

    barrier = pltpu.get_barrier_semaphore()

    def greet(device):
        pl.semaphore_signal(barrier, inc=1, device_id=device, device_id_type=MESH)

    greet({"shot": sibling})
    greet({"shot": partner})

    @pl.when(at_end)
    def _():
        greet({"shot": partner, "dom": inside})

    @pl.when(passes)
    def _():
        greet({"shot": partner, "dom": outside})

    @pl.when(has_low)
    def _():
        greet({"dom": dom - 1})

    @pl.when(has_high)
    def _():
        greet({"dom": dom + 1})

    loads = [
        pltpu.make_async_copy(labels_hbm, labels, load_sem.at[0]),
        pltpu.make_async_copy(near_hbm.at[0], aa.at[1], load_sem.at[1]),
        pltpu.make_async_copy(current_hbm.at[0], ue.at[0, pl.ds(4, planes)], load_sem.at[2]),
        pltpu.make_async_copy(before_hbm.at[0], u0, load_sem.at[3]),
        pltpu.make_async_copy(far_hbm.at[0], aa.at[0], load_sem.at[4]),
        pltpu.make_async_copy(table_hbm, table, load_sem.at[5]),
        pltpu.make_async_copy(source_hbm, source, load_sem.at[6]),
        pltpu.make_async_copy(wavelet_hbm, wavelet, load_sem.at[7]),
        pltpu.make_async_copy(receivers_hbm, receivers, load_sem.at[8]),
        pltpu.make_async_copy(residual_hbm, residual, load_sem.at[9]),
    ]
    for k in (5, 0, 1, 2, 3, 6, 7, 8, 9, 4):
        loads[k].start()

    peers = 2 + jnp.where(at_end | passes, 1, 0) + jnp.where(has_low, 1, 0) + jnp.where(has_high, 1, 0)
    pl.semaphore_wait(barrier, peers)

    def to_low(e, source_ref):
        buffer = ue.at[e] if e < 4 else se.at[e - 4]
        return pltpu.make_async_remote_copy(
            source_ref, buffer.at[pl.ds(planes + 4, 4)], send_sem.at[0, e], recv_sem.at[0, e],
            device_id={"dom": dom - 1}, device_id_type=MESH,
        )

    def to_high(e, source_ref):
        buffer = ue.at[e] if e < 4 else se.at[e - 4]
        return pltpu.make_async_remote_copy(
            source_ref, buffer.at[pl.ds(0, 4)], send_sem.at[1, e], recv_sem.at[1, e],
            device_id={"dom": dom + 1}, device_id_type=MESH,
        )

    def low_edge(e):
        if e == 0:
            return current_hbm.at[0, pl.ds(0, 4)]
        return (ue.at[e] if e < 4 else se.at[e - 4]).at[pl.ds(4, 4)]

    def high_edge(e):
        if e == 0:
            return current_hbm.at[0, pl.ds(planes - 4, 4)]
        return (ue.at[e] if e < 4 else se.at[e - 4]).at[pl.ds(planes, 4)]

    def send(e, high):
        @pl.when(jnp.logical_not(high) & has_low)
        def _():
            to_low(e, low_edge(e)).start()

        @pl.when(high & has_high)
        def _():
            to_high(e, high_edge(e)).start()

    def wait(e, high):
        @pl.when(jnp.logical_not(high) & has_low)
        def _():
            to_high(e, high_edge(e)).wait_recv()

        @pl.when(high & has_high)
        def _():
            to_low(e, low_edge(e)).wait_recv()

    order = (place == 0, place != 0)

    def edge_group(high):
        return jnp.where(high, groups - 1, 0)

    for high in order:
        send(0, high)

    @pl.when(dom == 0)
    def _():
        for e in range(4):
            ue[e, 0:4] = jnp.zeros((4, depth, across), F32)
            se[e, 0:4] = jnp.zeros((4, depth, across), F32)

    @pl.when(dom == doms - 1)
    def _():
        for e in range(4):
            ue[e, planes + 4:planes + 8] = jnp.zeros((4, depth, across), F32)
            se[e, planes + 4:planes + 8] = jnp.zeros((4, depth, across), F32)

    loads[5].wait()
    speeds = [table[k] * (1.0 / scale) for k in range(table.shape[0])]
    loads[0].wait()
    loads[1].wait()

    def first_plane(p):
        def rows(i, _):
            r = pl.ds(pl.multiple_of(i * 16, 16), 16)
            region = labels[p, r, :]
            speed = jnp.full(region.shape, speeds[0], F32)
            for k in range(1, len(speeds)):
                speed = jnp.where(region == k, speeds[k], speed)
            rate[p, r, :] = speed
            se[0, p + 4, r, :] = speed * aa[1, p, r, :]
            return 0

        lax.fori_loop(0, depth // 16, rows, 0)

    def first_group(base):
        lax.fori_loop(0, 4, lambda j, c: (first_plane(base + j), c)[1], 0)

    for high in order:
        first_group(4 * edge_group(high))
        send(4, high)
    lax.fori_loop(4, planes - 4, lambda p, c: (first_plane(p), c)[1], 0)

    row_band, column_band = band(across), band(depth)
    for k in range(3):
        along_y[k * across:(k + 1) * across, :] = row_band
        along_z[:, k * depth:(k + 1) * depth] = column_band

    for k in range(6, 10):
        loads[k].wait()
    row = lax.broadcasted_iota(jnp.int32, (depth, across), 0)
    column = lax.broadcasted_iota(jnp.int32, (depth, across), 1)
    spot[...] = jnp.where((row == source[0, 1]) & (column == source[0, 2]), 1.0, 0.0).astype(F32)
    source_plane = source[0, 0] - dom * planes

    def across_stage(ext, out):
        def pair(i, _):
            for h in range(2):
                g = 2 * i + h
                for q in range(4):
                    for part in range(depth // 16):
                        at = 16 * part
                        terms = split(ext[4 + 4 * g + q, at:at + 16, :])
                        for k in range(3):
                            wide[h, q * depth + at:q * depth + at + 16, k * across:(k + 1) * across] = terms[k]
                            tall[h, q, k * depth + at:k * depth + at + 16, :] = terms[k]
                in_y = jnp.dot(wide[h], along_y[...], preferred_element_type=F32)
                for q in range(4):
                    in_z = jnp.dot(along_z[...], tall[h, q], preferred_element_type=F32)
                    out[4 * g + q] = in_y[q * depth:(q + 1) * depth] + in_z
            return 0

        lax.fori_loop(0, groups // 2, pair, 0)

    def laplace(planes_of, j, rest):
        result = rest + centre * planes_of[j + 4]
        for k in range(1, 5):
            result = result + sides[k - 1] * (planes_of[j + 4 + k] + planes_of[j + 4 - k])
        return result

    def forward_group(n, g):
        pulses = [jnp.where(source_plane == 4 * g + j, wavelet[0, n], 0.0) for j in range(4)]

        def rows(i, _):
            r = pl.ds(pl.multiple_of(i * 8, 8), 8)
            window = [ue[n, 4 * g + q, r, :] for q in range(12)]
            for j in range(4):
                p = 4 * g + j
                curve = laplace(window, j, yzf[p, r, :])
                if n == 3:
                    grad[p, r, :] = grad[p, r, :] + aa[1, p, r, :] * curve
                else:
                    lap[n, p, r, :] = curve
                previous = u0[p, r, :] if n == 0 else ue[n - 1, p + 4, r, :]
                upcoming = 2.0 * window[j + 4] - previous + rate[p, r, :] * curve
                upcoming = upcoming + pulses[j] * spot[r, :]
                if n == 3:
                    final[0, p, r, :] = upcoming
                else:
                    ue[n + 1, p + 4, r, :] = upcoming
            return 0

        lax.fori_loop(0, depth // 8, rows, 0)

    def adjoint_group(m, g):
        def rows(i, _):
            r = pl.ds(pl.multiple_of(i * 8, 8), 8)
            window = [se[m, 4 * g + q, r, :] for q in range(12)]
            for j in range(4):
                p = 4 * g + j
                curve = laplace(window, j, yza[p, r, :])
                earlier = 2.0 * aa[m + 1, p, r, :] - aa[m, p, r, :] + curve + inject[3 - m, p, r, :]
                if m == 3:
                    first[0, p, r, :] = earlier
                else:
                    aa[m + 2, p, r, :] = earlier
                    se[m + 1, p + 4, r, :] = rate[p, r, :] * earlier
            return 0

        lax.fori_loop(0, depth // 8, rows, 0)

    def middle(one, n):
        lax.fori_loop(1, groups - 1, lambda g, c: (one(n, g), c)[1], 0)

    cell = (receivers[0] - dom * planes) * depth + receivers[1]

    def onehot_rows(i, _):
        at = pl.multiple_of(i * 16, 16)
        here = lax.broadcasted_iota(jnp.int32, (16, recs), 0) + at
        onehot[pl.ds(at, 16), :] = jnp.where(here == cell, 1.0, 0.0).astype(BF16)
        return 0

    lax.fori_loop(0, planes * depth // 16, onehot_rows, 0)

    def inject_step(n):
        value = residual[n:n + 1, :]
        high = value.astype(BF16).astype(F32)
        parts = (high, (value - high).astype(BF16).astype(F32))

        def columns(i, _):
            at = pl.multiple_of(i * 16, 16)
            here = lax.broadcasted_iota(jnp.int32, (16, recs), 0) + at == receivers[2]
            for k in range(2):
                amounts[pl.ds(pl.multiple_of(at + k * across, 16), 16), :] = jnp.where(here, parts[k], 0.0).astype(BF16)
            return 0

        lax.fori_loop(0, across // 16, columns, 0)

        def half(i, _):
            rows = pl.ds(pl.multiple_of(i * 8 * depth, 8 * depth), 8 * depth)
            spread = lax.dot_general(
                onehot[rows, :], amounts[...], (((1,), (1,)), ((), ())), preferred_element_type=F32
            )
            both = spread[:, across:] + spread[:, :across]
            inject[n, pl.ds(8 * i, 8)] = both.reshape(8, depth, across)
            return 0

        lax.fori_loop(0, planes // 8, half, 0)

    def combine(p, _):
        def rows(i, _):
            r = pl.ds(pl.multiple_of(i * 16, 16), 16)
            value = aa[2, p, r, :] * lap[2, p, r, :]
            for n in (1, 0):
                value = value + aa[4 - n, p, r, :] * lap[n, p, r, :]
            grad[p, r, :] = value
            return 0

        lax.fori_loop(0, depth // 16, rows, 0)
        return 0

    mine, other = 4 + 4 * core, 8 - 4 * core
    mine_edge, other_edge = (planes - 4) * core, (planes - 4) * (1 - core)

    def gradient_copy(phase, chunk, source_ref, target_ref, device):
        return pltpu.make_async_remote_copy(
            source_ref, target_ref, gsend_sem.at[phase, chunk], grecv_sem.at[phase, chunk],
            device_id=device, device_id_type=MESH,
        )

    def to_sibling():
        return gradient_copy(0, 0, grad.at[pl.ds(other, 4)], near_grad.at[pl.ds(0, 4)], {"shot": sibling})

    def to_partner():
        return gradient_copy(1, 0, partial.at[pl.ds(0, 4)], far_grad.at[pl.ds(0, 4)], {"shot": partner})

    def to_passer():
        return gradient_copy(3, 0, partial.at[pl.ds(0, 3)], passing, {"shot": partner, "dom": inside})

    def rest_to_partner():
        rest = pl.ds(3, 1)
        return gradient_copy(3, 1, partial.at[rest], far_grad.at[rest], {"shot": partner})

    def pass_on():
        return gradient_copy(4, 0, passing, far_grad.at[pl.ds(0, 3)], {"dom": outside})

    def total_to_sibling():
        place_of = gradient.at[pl.ds(mine, 4)]
        return gradient_copy(2, 0, place_of, place_of, {"shot": sibling})

    def edge_to_sibling(j):
        return gradient_copy(0, 1 + j, grad.at[other_edge + j], near_grad.at[4 + j], {"shot": sibling})

    def edge_to_partner(j):
        return gradient_copy(1, 1 + j, partial.at[4 + j], far_grad.at[4 + j], {"shot": partner})

    def edge_total_to_sibling(j):
        place_of = gradient.at[mine_edge + j]
        return gradient_copy(2, 1 + j, place_of, place_of, {"shot": sibling})

    def sum_near():
        to_sibling().wait_recv()

        def one(j, _):
            partial[j] = grad[mine + j] + near_grad[j]
            return 0

        lax.fori_loop(0, 4, one, 0)

        @pl.when(at_end)
        def _():
            to_passer().start()
            rest_to_partner().start()

        @pl.when(jnp.logical_not(at_end))
        def _():
            to_partner().start()

    def sum_far():
        @pl.when(at_end)
        def _():
            rest_to_partner().wait_recv()
            pass_on().wait_recv()

        @pl.when(jnp.logical_not(at_end))
        def _():
            to_partner().wait_recv()

        def one(j, _):
            gradient[mine + j] = (partial[j] + far_grad[j]) * (1.0 / scale)
            return 0

        lax.fori_loop(0, 4, one, 0)
        total_to_sibling().start()

    def sum_near_edge(high):
        owner = high == (core == 1)

        @pl.when(jnp.logical_not(owner))
        def _():
            for j in range(4):
                edge_to_sibling(j).start()

        @pl.when(owner)
        def _():
            for j in range(4):
                edge_to_sibling(j).wait_recv()
                partial[4 + j] = grad[mine_edge + j] + near_grad[4 + j]
                edge_to_partner(j).start()

    def sum_far_edge():
        for j in range(4):
            edge_to_partner(j).wait_recv()
            gradient[mine_edge + j] = (partial[4 + j] + far_grad[4 + j]) * (1.0 / scale)
            edge_total_to_sibling(j).start()

    loads[2].wait()
    across_stage(ue.at[0], yzf)
    loads[3].wait()
    middle(forward_group, 0)
    inject_step(3)
    loads[4].wait()
    across_stage(se.at[0], yza)
    middle(adjoint_group, 0)

    for n in range(4):
        for high in order:
            wait(n, high)
            forward_group(n, edge_group(high))
            if n < 3:
                send(n + 1, high)
            else:
                sum_near_edge(high)
        if n < 3:
            across_stage(ue.at[n + 1], yzf)
            if n == 2:
                lax.fori_loop(4, planes - 4, combine, 0)
            middle(forward_group, n + 1)
        if n == 2:
            to_sibling().start()
            sum_near()
        if n == 3:
            @pl.when(passes)
            def _():
                to_passer().wait_recv()
                pass_on().start()
        if n < 2:
            inject_step(2 - n)
        for high in order:
            wait(n + 4, high)
            adjoint_group(n, edge_group(high))
            if n < 3:
                send(n + 5, high)
        if n == 1:
            inject_step(0)
        if n < 3:
            across_stage(se.at[n + 1], yza)
            middle(adjoint_group, n + 1)
        if n == 2:
            lax.fori_loop(0, 4, combine, 0)
            lax.fori_loop(planes - 4, planes, combine, 0)
    sum_far_edge()
    sum_far()

    total_to_sibling().wait_recv()
    for j in range(4):
        edge_total_to_sibling(j).wait_recv()
    for e in range(8):
        @pl.when(has_low)
        def _():
            to_low(e, low_edge(e)).wait_send()

        @pl.when(has_high)
        def _():
            to_high(e, high_edge(e)).wait_send()
    to_sibling().wait_send()
    total_to_sibling().wait_send()

    @pl.when(at_end)
    def _():
        to_passer().wait_send()
        rest_to_partner().wait_send()

    @pl.when(passes)
    def _():
        pass_on().wait_send()

    @pl.when(jnp.logical_not(at_end))
    def _():
        to_partner().wait_send()

    for j in range(4):
        edge_to_sibling(j).wait_send()
        edge_to_partner(j).wait_send()
        edge_total_to_sibling(j).wait_send()


def write(*refs):
    sems = refs[6]
    copies = []
    for k in range(3):
        source_ref, target_ref = refs[k], refs[k + 3]
        if k < 2:
            source_ref, target_ref = source_ref.at[0], target_ref.at[0]
        size = source_ref.shape[0] // 4
        for part in range(4):
            piece = pl.ds(part * size, size)
            copies.append(pltpu.make_async_copy(source_ref.at[piece], target_ref.at[piece], sems.at[k, part]))
    for copy in copies:
        copy.start()
    for copy in copies:
        copy.wait()


def per_device(
    doms, wave_before, wave_current, adjoint_far, adjoint_near, labels, table,
    source_index, wavelet, receiver_index, residual,
):
    block = wave_current.shape
    planes, depth, across = labels.shape
    recs = receiver_index.shape[1]
    field = (planes, depth, across)
    extended = (4, planes + 8, depth, across)
    whole = pl.BlockSpec(memory_space=pltpu.HBM)
    vectors = pl.BlockSpec(memory_space=pltpu.VMEM)
    results = pl.pallas_call(
        functools.partial(kernel, doms),
        out_shape=(
            pltpu.VMEM(block, F32),
            pltpu.VMEM(block, F32),
            pltpu.VMEM(field, F32),
        ),
        in_specs=[whole] * 10,
        out_specs=(vectors, vectors, vectors),
        scratch_shapes=[
            pltpu.SMEM(table.shape, F32),
            pltpu.SMEM(source_index.shape, jnp.int32),
            pltpu.SMEM(wavelet.shape, F32),
            pltpu.VMEM((3, 1, recs), jnp.int32),
            pltpu.VMEM(residual.shape[1:], F32),
            pltpu.VMEM(extended, F32),
            pltpu.VMEM(field, F32),
            pltpu.VMEM(extended, F32),
            pltpu.VMEM((5,) + field, F32),
            pltpu.VMEM((3,) + field, F32),
            pltpu.VMEM(field, F32),
            pltpu.VMEM(field, jnp.int32),
            pltpu.VMEM(field, F32),
            pltpu.VMEM(field, F32),
            pltpu.VMEM((2, 4 * depth, 3 * across), BF16),
            pltpu.VMEM((2, 4, 3 * depth, across), BF16),
            pltpu.VMEM((3 * across, across), BF16),
            pltpu.VMEM((depth, 3 * depth), BF16),
            pltpu.VMEM((planes * depth, recs), BF16),
            pltpu.VMEM((2 * across, recs), BF16),
            pltpu.VMEM((4,) + field, F32),
            pltpu.VMEM((depth, across), F32),
            pltpu.VMEM(field, F32),
            pltpu.VMEM((8, depth, across), F32),
            pltpu.VMEM((8, depth, across), F32),
            pltpu.VMEM((8, depth, across), F32),
            pltpu.VMEM((3, depth, across), F32),
            pltpu.SemaphoreType.DMA((10,)),
            pltpu.SemaphoreType.DMA((2, 8)),
            pltpu.SemaphoreType.DMA((2, 8)),
            pltpu.SemaphoreType.DMA((5, 5)),
            pltpu.SemaphoreType.DMA((5, 5)),
        ],
        compiler_params=pltpu.CompilerParams(
            collective_id=0, has_side_effects=True, vmem_limit_bytes=60 << 20
        ),
        name="window",
    )(
        wave_before, wave_current, adjoint_far, adjoint_near, labels, table,
        source_index, wavelet, jnp.transpose(receiver_index, (2, 0, 1)), residual[0],
    )
    held = [pltpu.with_memory_space_constraint(result, pltpu.VMEM) for result in results]
    return pl.pallas_call(
        write,
        out_shape=tuple(jax.ShapeDtypeStruct(result.shape, F32) for result in results),
        in_specs=[vectors] * 3,
        out_specs=(whole,) * 3,
        scratch_shapes=[pltpu.SemaphoreType.DMA((3, 4))],
        compiler_params=pltpu.CompilerParams(vmem_limit_bytes=1 << 20),
        name="write",
    )(*held)


def solution(mesh):
    fields = P("shot", "dom", None, None)
    return jax.shard_map(
        functools.partial(per_device, mesh.shape["dom"]),
        mesh=mesh,
        in_specs=(
            fields, fields, fields, fields, P("dom", None, None), P(),
            P("shot", None), P("shot", None), P("shot", None, None), P("shot", None, None),
        ),
        out_specs=(fields, fields, P("dom", None, None)),
        check_vma=False,
    )
```

```python
import functools

import jax
import jax.numpy as jnp
import numpy as np
from jax import lax
from jax.experimental import pallas as pl
from jax.experimental.pallas import tpu as pltpu
from jax.sharding import PartitionSpec as P

MESH = pl.DeviceIdType.MESH
F32 = jnp.float32
BF16 = jnp.bfloat16

ring = 8

scale = 5040.0
centre = 3.0 * -14350.0
sides = (8064.0, -1008.0, 128.0, -9.0)


def split(values):
    high = values.astype(BF16)
    rest = values - high.astype(F32)
    middle = rest.astype(BF16)
    low = (rest - middle.astype(F32)).astype(BF16)
    return high, middle, low


def band(size):
    row = lax.broadcasted_iota(jnp.int32, (size, size), 0)
    column = lax.broadcasted_iota(jnp.int32, (size, size), 1)
    away = jnp.abs(row - column)
    result = jnp.zeros((size, size), F32)
    for k in range(1, 5):
        result = jnp.where(away == k, sides[k - 1], result)
    return result.astype(BF16)


def kernel(
    doms,
    before_hbm, current_hbm, far_hbm, near_hbm, labels_hbm,
    table_hbm, source_hbm, wavelet_hbm, receivers_hbm, residual_hbm,
    final, first, gradient,
    table, source, wavelet, receivers, residual, ue, u0, se, aa, lap, rate, labels, yzf, yza, wide, tall, along_y, along_z,
    onehot, amounts, inject, spot, grad, near_grad, far_grad, partial, passing,
    load_sem, send_sem, recv_sem, gsend_sem, grecv_sem,
):
    shot = lax.axis_index("shot")
    dom = lax.axis_index("dom")
    planes, depth, across = u0.shape
    groups = planes // 4
    recs = receivers.shape[2]
    core = lax.rem(shot, 2)
    sibling = shot + 1 - 2 * core
    partner = lax.rem(shot + 2, 4)
    place = lax.rem(dom, ring)
    at_end = (place == 0) | (place == ring - 1)
    passes = (place == 1) | (place == ring - 2)
    inside = jnp.where(place == 0, dom + 1, dom - 1)
    outside = jnp.where(place == 1, dom - 1, dom + 1)
    has_low = dom > 0
    has_high = dom < doms - 1

    barrier = pltpu.get_barrier_semaphore()

    def greet(device):
        pl.semaphore_signal(barrier, inc=1, device_id=device, device_id_type=MESH)

    greet({"shot": sibling})
    greet({"shot": partner})

    @pl.when(at_end)
    def _():
        greet({"shot": partner, "dom": inside})

    @pl.when(passes)
    def _():
        greet({"shot": partner, "dom": outside})

    @pl.when(has_low)
    def _():
        greet({"dom": dom - 1})

    @pl.when(has_high)
    def _():
        greet({"dom": dom + 1})

    loads = [
        pltpu.make_async_copy(labels_hbm, labels, load_sem.at[0]),
        pltpu.make_async_copy(near_hbm.at[0], aa.at[1], load_sem.at[1]),
        pltpu.make_async_copy(current_hbm.at[0], ue.at[0, pl.ds(4, planes)], load_sem.at[2]),
        pltpu.make_async_copy(before_hbm.at[0], u0, load_sem.at[3]),
        pltpu.make_async_copy(far_hbm.at[0], aa.at[0], load_sem.at[4]),
        pltpu.make_async_copy(table_hbm, table, load_sem.at[5]),
        pltpu.make_async_copy(source_hbm, source, load_sem.at[6]),
        pltpu.make_async_copy(wavelet_hbm, wavelet, load_sem.at[7]),
        pltpu.make_async_copy(receivers_hbm, receivers, load_sem.at[8]),
        pltpu.make_async_copy(residual_hbm, residual, load_sem.at[9]),
    ]
    for k in (5, 0, 1, 2, 3, 6, 7, 8, 9, 4):
        loads[k].start()

    peers = 2 + jnp.where(at_end | passes, 1, 0) + jnp.where(has_low, 1, 0) + jnp.where(has_high, 1, 0)
    pl.semaphore_wait(barrier, peers)

    def to_low(e, source_ref):
        buffer = ue.at[e] if e < 4 else se.at[e - 4]
        return pltpu.make_async_remote_copy(
            source_ref, buffer.at[pl.ds(planes + 4, 4)], send_sem.at[0, e], recv_sem.at[0, e],
            device_id={"dom": dom - 1}, device_id_type=MESH,
        )

    def to_high(e, source_ref):
        buffer = ue.at[e] if e < 4 else se.at[e - 4]
        return pltpu.make_async_remote_copy(
            source_ref, buffer.at[pl.ds(0, 4)], send_sem.at[1, e], recv_sem.at[1, e],
            device_id={"dom": dom + 1}, device_id_type=MESH,
        )

    def low_edge(e):
        if e == 0:
            return current_hbm.at[0, pl.ds(0, 4)]
        return (ue.at[e] if e < 4 else se.at[e - 4]).at[pl.ds(4, 4)]

    def high_edge(e):
        if e == 0:
            return current_hbm.at[0, pl.ds(planes - 4, 4)]
        return (ue.at[e] if e < 4 else se.at[e - 4]).at[pl.ds(planes, 4)]

    def send(e, high):
        @pl.when(jnp.logical_not(high) & has_low)
        def _():
            to_low(e, low_edge(e)).start()

        @pl.when(high & has_high)
        def _():
            to_high(e, high_edge(e)).start()

    def wait(e, high):
        @pl.when(jnp.logical_not(high) & has_low)
        def _():
            to_high(e, high_edge(e)).wait_recv()

        @pl.when(high & has_high)
        def _():
            to_low(e, low_edge(e)).wait_recv()

    order = (place == 0, place != 0)

    def edge_group(high):
        return jnp.where(high, groups - 1, 0)

    for high in order:
        send(0, high)

    @pl.when(dom == 0)
    def _():
        for e in range(4):
            ue[e, 0:4] = jnp.zeros((4, depth, across), F32)
            se[e, 0:4] = jnp.zeros((4, depth, across), F32)

    @pl.when(dom == doms - 1)
    def _():
        for e in range(4):
            ue[e, planes + 4:planes + 8] = jnp.zeros((4, depth, across), F32)
            se[e, planes + 4:planes + 8] = jnp.zeros((4, depth, across), F32)

    loads[5].wait()
    speeds = [table[k] * (1.0 / scale) for k in range(table.shape[0])]
    loads[0].wait()
    loads[1].wait()

    def first_plane(p):
        def rows(i, _):
            r = pl.ds(pl.multiple_of(i * 16, 16), 16)
            region = labels[p, r, :]
            speed = jnp.full(region.shape, speeds[0], F32)
            for k in range(1, len(speeds)):
                speed = jnp.where(region == k, speeds[k], speed)
            rate[p, r, :] = speed
            se[0, p + 4, r, :] = speed * aa[1, p, r, :]
            return 0

        lax.fori_loop(0, depth // 16, rows, 0)

    def first_group(base):
        lax.fori_loop(0, 4, lambda j, c: (first_plane(base + j), c)[1], 0)

    for high in order:
        first_group(4 * edge_group(high))
        send(4, high)
    lax.fori_loop(4, planes - 4, lambda p, c: (first_plane(p), c)[1], 0)

    row_band, column_band = band(across), band(depth)
    for k in range(3):
        along_y[k * across:(k + 1) * across, :] = row_band
        along_z[:, k * depth:(k + 1) * depth] = column_band

    for k in range(6, 10):
        loads[k].wait()
    row = lax.broadcasted_iota(jnp.int32, (depth, across), 0)
    column = lax.broadcasted_iota(jnp.int32, (depth, across), 1)
    spot[...] = jnp.where((row == source[0, 1]) & (column == source[0, 2]), 1.0, 0.0).astype(F32)
    source_plane = source[0, 0] - dom * planes

    def across_stage(ext, out):
        def pair(i, _):
            for h in range(2):
                g = 2 * i + h
                for q in range(4):
                    for part in range(depth // 16):
                        at = 16 * part
                        terms = split(ext[4 + 4 * g + q, at:at + 16, :])
                        for k in range(3):
                            wide[h, q * depth + at:q * depth + at + 16, k * across:(k + 1) * across] = terms[k]
                            tall[h, q, k * depth + at:k * depth + at + 16, :] = terms[k]
                in_y = jnp.dot(wide[h], along_y[...], preferred_element_type=F32)
                for q in range(4):
                    in_z = jnp.dot(along_z[...], tall[h, q], preferred_element_type=F32)
                    out[4 * g + q] = in_y[q * depth:(q + 1) * depth] + in_z
            return 0

        lax.fori_loop(0, groups // 2, pair, 0)

    def laplace(planes_of, j, rest):
        result = rest + centre * planes_of[j + 4]
        for k in range(1, 5):
            result = result + sides[k - 1] * (planes_of[j + 4 + k] + planes_of[j + 4 - k])
        return result

    def forward_group(n, g):
        pulses = [jnp.where(source_plane == 4 * g + j, wavelet[0, n], 0.0) for j in range(4)]

        def rows(i, _):
            r = pl.ds(pl.multiple_of(i * 8, 8), 8)
            window = [ue[n, 4 * g + q, r, :] for q in range(12)]
            for j in range(4):
                p = 4 * g + j
                curve = laplace(window, j, yzf[p, r, :])
                if n == 3:
                    grad[p, r, :] = grad[p, r, :] + aa[1, p, r, :] * curve
                else:
                    lap[n, p, r, :] = curve
                previous = u0[p, r, :] if n == 0 else ue[n - 1, p + 4, r, :]
                upcoming = 2.0 * window[j + 4] - previous + rate[p, r, :] * curve
                upcoming = upcoming + pulses[j] * spot[r, :]
                if n == 3:
                    final[0, p, r, :] = upcoming
                else:
                    ue[n + 1, p + 4, r, :] = upcoming
            return 0

        lax.fori_loop(0, depth // 8, rows, 0)

    def adjoint_group(m, g):
        def rows(i, _):
            r = pl.ds(pl.multiple_of(i * 8, 8), 8)
            window = [se[m, 4 * g + q, r, :] for q in range(12)]
            for j in range(4):
                p = 4 * g + j
                curve = laplace(window, j, yza[p, r, :])
                earlier = 2.0 * aa[m + 1, p, r, :] - aa[m, p, r, :] + curve + inject[3 - m, p, r, :]
                if m == 3:
                    first[0, p, r, :] = earlier
                else:
                    aa[m + 2, p, r, :] = earlier
                    se[m + 1, p + 4, r, :] = rate[p, r, :] * earlier
            return 0

        lax.fori_loop(0, depth // 8, rows, 0)

    def middle(one, n):
        lax.fori_loop(1, groups - 1, lambda g, c: (one(n, g), c)[1], 0)

    cell = (receivers[0] - dom * planes) * depth + receivers[1]

    def onehot_rows(i, _):
        at = pl.multiple_of(i * 16, 16)
        here = lax.broadcasted_iota(jnp.int32, (16, recs), 0) + at
        onehot[pl.ds(at, 16), :] = jnp.where(here == cell, 1.0, 0.0).astype(BF16)
        return 0

    lax.fori_loop(0, planes * depth // 16, onehot_rows, 0)

    def inject_step(n):
        value = residual[n:n + 1, :]
        high = value.astype(BF16).astype(F32)
        parts = (high, (value - high).astype(BF16).astype(F32))

        def columns(i, _):
            at = pl.multiple_of(i * 16, 16)
            here = lax.broadcasted_iota(jnp.int32, (16, recs), 0) + at == receivers[2]
            for k in range(2):
                amounts[pl.ds(pl.multiple_of(at + k * across, 16), 16), :] = jnp.where(here, parts[k], 0.0).astype(BF16)
            return 0

        lax.fori_loop(0, across // 16, columns, 0)

        def half(i, _):
            rows = pl.ds(pl.multiple_of(i * 8 * depth, 8 * depth), 8 * depth)
            spread = lax.dot_general(
                onehot[rows, :], amounts[...], (((1,), (1,)), ((), ())), preferred_element_type=F32
            )
            both = spread[:, across:] + spread[:, :across]
            inject[n, pl.ds(8 * i, 8)] = both.reshape(8, depth, across)
            return 0

        lax.fori_loop(0, planes // 8, half, 0)

    def combine(p, _):
        def rows(i, _):
            r = pl.ds(pl.multiple_of(i * 16, 16), 16)
            value = aa[2, p, r, :] * lap[2, p, r, :]
            for n in (1, 0):
                value = value + aa[4 - n, p, r, :] * lap[n, p, r, :]
            grad[p, r, :] = value
            return 0

        lax.fori_loop(0, depth // 16, rows, 0)
        return 0

    mine, other = 4 + 4 * core, 8 - 4 * core
    mine_edge, other_edge = (planes - 4) * core, (planes - 4) * (1 - core)

    def gradient_copy(phase, chunk, source_ref, target_ref, device):
        return pltpu.make_async_remote_copy(
            source_ref, target_ref, gsend_sem.at[phase, chunk], grecv_sem.at[phase, chunk],
            device_id=device, device_id_type=MESH,
        )

    def to_sibling():
        return gradient_copy(0, 0, grad.at[pl.ds(other, 4)], near_grad.at[pl.ds(0, 4)], {"shot": sibling})

    def to_partner():
        return gradient_copy(1, 0, partial.at[pl.ds(0, 4)], far_grad.at[pl.ds(0, 4)], {"shot": partner})

    def to_passer():
        return gradient_copy(3, 0, partial.at[pl.ds(0, 3)], passing, {"shot": partner, "dom": inside})

    def rest_to_partner():
        rest = pl.ds(3, 1)
        return gradient_copy(3, 1, partial.at[rest], far_grad.at[rest], {"shot": partner})

    def pass_on():
        return gradient_copy(4, 0, passing, far_grad.at[pl.ds(0, 3)], {"dom": outside})

    def total_to_sibling():
        place_of = gradient.at[pl.ds(mine, 4)]
        return gradient_copy(2, 0, place_of, place_of, {"shot": sibling})

    def edge_to_sibling(j):
        return gradient_copy(0, 1 + j, grad.at[other_edge + j], near_grad.at[4 + j], {"shot": sibling})

    def edge_to_partner(j):
        return gradient_copy(1, 1 + j, partial.at[4 + j], far_grad.at[4 + j], {"shot": partner})

    def edge_total_to_sibling(j):
        place_of = gradient.at[mine_edge + j]
        return gradient_copy(2, 1 + j, place_of, place_of, {"shot": sibling})

    def sum_near():
        to_sibling().wait_recv()

        def one(j, _):
            partial[j] = grad[mine + j] + near_grad[j]
            return 0

        lax.fori_loop(0, 4, one, 0)

        @pl.when(at_end)
        def _():
            to_passer().start()

        @pl.when(jnp.logical_not(at_end))
        def _():
            to_partner().start()

    def sum_far():
        @pl.when(at_end)
        def _():
            rest_to_partner().wait_recv()
            pass_on().wait_recv()

        @pl.when(jnp.logical_not(at_end))
        def _():
            to_partner().wait_recv()

        def one(j, _):
            gradient[mine + j] = (partial[j] + far_grad[j]) * (1.0 / scale)
            return 0

        lax.fori_loop(0, 4, one, 0)
        total_to_sibling().start()

    def sum_near_edge(high):
        owner = high == (core == 1)

        @pl.when(jnp.logical_not(owner))
        def _():
            for j in range(4):
                edge_to_sibling(j).start()

        @pl.when(owner)
        def _():
            for j in range(4):
                edge_to_sibling(j).wait_recv()
                partial[4 + j] = grad[mine_edge + j] + near_grad[4 + j]
                edge_to_partner(j).start()

    def sum_far_edge():
        for j in range(4):
            edge_to_partner(j).wait_recv()
            gradient[mine_edge + j] = (partial[4 + j] + far_grad[4 + j]) * (1.0 / scale)
            edge_total_to_sibling(j).start()

    loads[2].wait()
    across_stage(ue.at[0], yzf)
    loads[3].wait()
    middle(forward_group, 0)
    inject_step(3)
    loads[4].wait()
    across_stage(se.at[0], yza)
    middle(adjoint_group, 0)

    for n in range(4):
        for high in order:
            wait(n, high)
            forward_group(n, edge_group(high))
            if n < 3:
                send(n + 1, high)
            else:
                sum_near_edge(high)
        if n < 3:
            across_stage(ue.at[n + 1], yzf)
            if n == 2:
                lax.fori_loop(4, planes - 4, combine, 0)
            middle(forward_group, n + 1)
        if n == 2:
            to_sibling().start()
            sum_near()
        if n == 3:
            @pl.when(at_end)
            def _():
                rest_to_partner().start()

            @pl.when(passes)
            def _():
                to_passer().wait_recv()
                pass_on().start()
        if n < 2:
            inject_step(2 - n)
        for high in order:
            wait(n + 4, high)
            adjoint_group(n, edge_group(high))
            if n < 3:
                send(n + 5, high)
        if n == 1:
            inject_step(0)
        if n < 3:
            across_stage(se.at[n + 1], yza)
            middle(adjoint_group, n + 1)
        if n == 2:
            lax.fori_loop(0, 4, combine, 0)
            lax.fori_loop(planes - 4, planes, combine, 0)
    sum_far_edge()
    sum_far()

    total_to_sibling().wait_recv()
    for j in range(4):
        edge_total_to_sibling(j).wait_recv()
    for e in range(8):
        @pl.when(has_low)
        def _():
            to_low(e, low_edge(e)).wait_send()

        @pl.when(has_high)
        def _():
            to_high(e, high_edge(e)).wait_send()
    to_sibling().wait_send()
    total_to_sibling().wait_send()

    @pl.when(at_end)
    def _():
        to_passer().wait_send()
        rest_to_partner().wait_send()

    @pl.when(passes)
    def _():
        pass_on().wait_send()

    @pl.when(jnp.logical_not(at_end))
    def _():
        to_partner().wait_send()

    for j in range(4):
        edge_to_sibling(j).wait_send()
        edge_to_partner(j).wait_send()
        edge_total_to_sibling(j).wait_send()


def write(*refs):
    sems = refs[6]
    copies = []
    for k in range(3):
        source_ref, target_ref = refs[k], refs[k + 3]
        if k < 2:
            source_ref, target_ref = source_ref.at[0], target_ref.at[0]
        size = source_ref.shape[0] // 4
        for part in range(4):
            piece = pl.ds(part * size, size)
            copies.append(pltpu.make_async_copy(source_ref.at[piece], target_ref.at[piece], sems.at[k, part]))
    for copy in copies:
        copy.start()
    for copy in copies:
        copy.wait()


def per_device(
    doms, wave_before, wave_current, adjoint_far, adjoint_near, labels, table,
    source_index, wavelet, receiver_index, residual,
):
    block = wave_current.shape
    planes, depth, across = labels.shape
    recs = receiver_index.shape[1]
    field = (planes, depth, across)
    extended = (4, planes + 8, depth, across)
    whole = pl.BlockSpec(memory_space=pltpu.HBM)
    vectors = pl.BlockSpec(memory_space=pltpu.VMEM)
    results = pl.pallas_call(
        functools.partial(kernel, doms),
        out_shape=(
            pltpu.VMEM(block, F32),
            pltpu.VMEM(block, F32),
            pltpu.VMEM(field, F32),
        ),
        in_specs=[whole] * 10,
        out_specs=(vectors, vectors, vectors),
        scratch_shapes=[
            pltpu.SMEM(table.shape, F32),
            pltpu.SMEM(source_index.shape, jnp.int32),
            pltpu.SMEM(wavelet.shape, F32),
            pltpu.VMEM((3, 1, recs), jnp.int32),
            pltpu.VMEM(residual.shape[1:], F32),
            pltpu.VMEM(extended, F32),
            pltpu.VMEM(field, F32),
            pltpu.VMEM(extended, F32),
            pltpu.VMEM((5,) + field, F32),
            pltpu.VMEM((3,) + field, F32),
            pltpu.VMEM(field, F32),
            pltpu.VMEM(field, jnp.int32),
            pltpu.VMEM(field, F32),
            pltpu.VMEM(field, F32),
            pltpu.VMEM((2, 4 * depth, 3 * across), BF16),
            pltpu.VMEM((2, 4, 3 * depth, across), BF16),
            pltpu.VMEM((3 * across, across), BF16),
            pltpu.VMEM((depth, 3 * depth), BF16),
            pltpu.VMEM((planes * depth, recs), BF16),
            pltpu.VMEM((2 * across, recs), BF16),
            pltpu.VMEM((4,) + field, F32),
            pltpu.VMEM((depth, across), F32),
            pltpu.VMEM(field, F32),
            pltpu.VMEM((8, depth, across), F32),
            pltpu.VMEM((8, depth, across), F32),
            pltpu.VMEM((8, depth, across), F32),
            pltpu.VMEM((3, depth, across), F32),
            pltpu.SemaphoreType.DMA((10,)),
            pltpu.SemaphoreType.DMA((2, 8)),
            pltpu.SemaphoreType.DMA((2, 8)),
            pltpu.SemaphoreType.DMA((5, 5)),
            pltpu.SemaphoreType.DMA((5, 5)),
        ],
        compiler_params=pltpu.CompilerParams(
            collective_id=0, has_side_effects=True, vmem_limit_bytes=60 << 20
        ),
        name="window",
    )(
        wave_before, wave_current, adjoint_far, adjoint_near, labels, table,
        source_index, wavelet, jnp.transpose(receiver_index, (2, 0, 1)), residual[0],
    )
    held = [pltpu.with_memory_space_constraint(result, pltpu.VMEM) for result in results]
    return pl.pallas_call(
        write,
        out_shape=tuple(jax.ShapeDtypeStruct(result.shape, F32) for result in results),
        in_specs=[vectors] * 3,
        out_specs=(whole,) * 3,
        scratch_shapes=[pltpu.SemaphoreType.DMA((3, 4))],
        compiler_params=pltpu.CompilerParams(vmem_limit_bytes=1 << 20),
        name="write",
    )(*held)


def solution(mesh):
    fields = P("shot", "dom", None, None)
    return jax.shard_map(
        functools.partial(per_device, mesh.shape["dom"]),
        mesh=mesh,
        in_specs=(
            fields, fields, fields, fields, P("dom", None, None), P(),
            P("shot", None), P("shot", None), P("shot", None, None), P("shot", None, None),
        ),
        out_specs=(fields, fields, P("dom", None, None)),
        check_vma=False,
    )
```
